256 devices in a mesh: guide: 2 (over core), row: 32 (over x, z), col: 4 (over y).
Axes of the slice: x: 4, y: 4, z: 8, core: 2. Of those that a mesh axis runs over, the one named last changes fastest.
Arguments:
- hidden: bfloat16 [2, 16, 2048], P('guide', None, 'row')
- lengths: int32 [2, 16], P('guide'), may hold values from 2 to 4096, as said below
- kv_cache: bfloat16 [2, 16, 2, 4096, 512], P('guide', None, None, 'row', 'col'), as said below
- attn_gain: bfloat16 [2048], P('row'), may hold values from 0.5 to 1.5
- w_query: bfloat16 [2048, 2048], P('row', 'col'), may hold values from -0.125 to 0.125
- w_key_value: bfloat16 [2048, 2, 512], P('row', None, 'col'), may hold values from -0.125 to 0.125
- w_out: bfloat16 [2048, 2048], P('col', 'row'), may hold values from -0.125 to 0.125
- mlp_gain: bfloat16 [2048], P('row'), may hold values from 0.5 to 1.5
- w_gate_up: bfloat16 [2048, 2, 8192], P('row', None, 'col'), may hold values from -0.125 to 0.125
- w_down: bfloat16 [8192, 2048], P('col', 'row'), may hold values from -0.0625 to 0.0625
- final_gain: bfloat16 [2048], P('row'), may hold values from 0.5 to 1.5
- w_head: bfloat16 [2048, 128256], P('row', 'col'), may hold values from -0.25 to 0.25
- next_gain: bfloat16 [2048], P('row'), may hold values from 0.5 to 1.5
- w_next_query: bfloat16 [2048, 2048], P('row', 'col'), may hold values from -0.125 to 0.125
- w_next_kv: bfloat16 [2048, 2, 512], P('row', None, 'col'), may hold values from -0.125 to 0.125
- tenant: int32 [16], replicated, may hold values from 0 to 3
- guide_scale: float32 [4], replicated, may hold values from 1.5 to 6
Outputs:
- guided_logits: float32 [16, 128256], P('guide', ('col', 'row'))
- next_query: bfloat16 [2, 16, 2048], P('guide', None, 'col')
- next_key_value: bfloat16 [2, 16, 2, 512], P('guide', None, None, 'col')
The draws below stay inside these ranges and needn't reach their ends.
Inputs may be any that keep to these rules, and one draw needn't show every extreme that they name: `lengths`: in each group one request has exactly 4096 cached positions. `kv_cache`: keys (index 0 of the third dimension) are stored with the rotary embedding of their positions; values at index 1.
All inputs are finite; a program needn't handle non-finite values.
Results may differ from the reference program's by a relative error of at most 0.013.
Values may be sent and summed in bfloat16 or wider, within the bound.
No kernel may reach another device: no remote copies, remote signals or barrier semaphores. Data moves between devices by JAX's collectives and lax.ppermute only.
A program may use at most 64 MiB of HBM per device.

```python
import math
import jax
import jax.numpy as jnp
from jax import lax

D = 2048
HEADS = 32
KVH = 8
HD = 64
FF = 8192
V = 128256
REQ = 16
TENANTS = 4
QW = 2048
KVW = 512
MAXLEN = 4096


def draw_hidden(key, part):
    full_shape = (2, REQ, D)
    drawn = jax.random.normal(key, full_shape, jnp.float32)
    column_ramp = jnp.exp(jnp.log(3.0) * jnp.arange(D, dtype=jnp.float32) / D)
    drawn = drawn * column_ramp
    return drawn.astype(jnp.bfloat16)


def draw_lengths(key, part):
    upper = jax.random.randint(jax.random.fold_in(key, 37), (2, REQ), 3, MAXLEN + 1)
    drawn = jax.random.randint(key, (2, REQ), 2, upper)
    longest = jax.random.randint(jax.random.fold_in(key, 31), (2, 1), 0, REQ)
    return jnp.where(jnp.arange(REQ)[None, :] == longest, MAXLEN, drawn).astype(jnp.int32)


def draw_kv_cache(key, part):
    full_shape = (2, REQ, 2, MAXLEN, KVW)
    which = jnp.arange(2).reshape(1, 1, 2, 1, 1)
    slot = jnp.arange(MAXLEN).reshape(1, 1, 1, MAXLEN, 1)
    spread = jnp.where(which == 0, 1.5, 1.0)
    common = jax.random.normal(jax.random.fold_in(key, 41), (2, REQ, 1, 1, KVW), jnp.float32)
    drawn = jax.random.normal(key, full_shape, jnp.float32) * spread
    ramp = 0.6 * jnp.exp(jnp.log(4.0) * slot.astype(jnp.float32) / MAXLEN)
    drawn = drawn + jnp.where(which == 1, ramp * common, 0.0)
    return drawn.astype(jnp.bfloat16)


def touch_ends(entries, key, smallest, top_value):
    extent = entries.shape
    place = [jax.random.randint(jax.random.fold_in(key, axis), (), 0, extent[axis]) for axis in range(len(extent))]
    entries = entries.at[tuple(place)].set(smallest)
    longest = extent.index(max(extent))
    place[longest] = (place[longest] + 1) % extent[longest]
    return entries.at[tuple(place)].set(top_value)


def raised(drawn, stream_key, source, target, parts, factor):
    owner, partner = [(jnp.arange(drawn.shape[axis_at]) // (drawn.shape[axis_at] // parts)).reshape([-1 if axis == axis_at else 1 for axis in range(drawn.ndim)]) for axis_at in (source, target)]
    chosen = jax.random.permutation(stream_key, parts)[partner]
    strong = (owner == chosen) | (owner == (partner + parts // 2) % parts)
    return jnp.where(strong, factor * drawn, drawn)


def block_levels(stream_key, extent, split, least, largest):
    def one(dim, shards_of):
        draws = jax.random.uniform(jax.random.fold_in(jax.random.fold_in(stream_key, 6), dim), (shards_of,), jnp.float32, least / len(split), largest / len(split))
        return jnp.repeat(jnp.exp(draws), extent[dim] // shards_of).reshape((-1,) + (1,) * (len(extent) - dim - 1))

    loudness = one(*split[0])
    for cut in split[1:]:
        loudness = loudness * one(*cut)
    return loudness


def gaussian(own_key, extent, deviation, limit, split=(), kind=jnp.bfloat16):
    factor_of = block_levels(own_key, extent, split, -0.22, 0.18) if split else 1.0
    drawn = jax.random.normal(own_key, extent, jnp.float32) * deviation * factor_of
    return jnp.minimum(jnp.maximum(drawn, -limit), limit).astype(kind)


def bell_draw_with(stream_key, shape, scale, most, pieces, heavy, held_as=jnp.bfloat16):
    drawn = scale * jax.random.normal(stream_key, shape, jnp.float32)
    if pieces:
        drawn = drawn * block_levels(stream_key, shape, pieces, -0.22, 0.18)
    return jnp.clip(raised(drawn, jax.random.fold_in(stream_key, 3), *heavy), -most, most).astype(held_as)


def setup_inputs(seed: int = 0) -> dict:
    keys = jax.random.split(jax.random.key(seed), 18)
    hidden = draw_hidden(jax.random.fold_in(keys[17], 71), 0)
    lengths = draw_lengths(jax.random.fold_in(keys[17], 71), 0)
    kv_cache = draw_kv_cache(jax.random.fold_in(keys[17], 71), 0)
    attn_gain = jnp.clip(1.0 + 0.1 * jax.random.normal(keys[3], (D,), jnp.float32), 0.5, 1.5).astype(jnp.bfloat16)
    w_query = gaussian(keys[4], (D, QW), D ** -0.5, 0.125, ((0, 32), (1, 4)))
    w_key_value = gaussian(keys[5], (D, 2, KVW), D ** -0.5, 0.125, ((0, 32), (2, 4)))
    w_out = gaussian(keys[6], (QW, D), QW ** -0.5, 0.125, ((0, 4), (1, 32)))
    mlp_gain = jnp.clip(1.0 + 0.1 * jax.random.normal(keys[7], (D,), jnp.float32), 0.5, 1.5).astype(jnp.bfloat16)
    w_gate_up = gaussian(keys[8], (D, 2, FF), D ** -0.5, 0.125, ((0, 32), (2, 4)))
    w_down = gaussian(keys[9], (FF, D), FF ** -0.5, 0.0625, ((0, 4), (1, 32)))
    final_gain = jnp.clip(1.0 + 0.1 * jax.random.normal(keys[10], (D,), jnp.float32), 0.5, 1.5).astype(jnp.bfloat16)
    w_head = bell_draw_with(keys[11], (D, V), D ** -0.5, 0.25, ((0, 32), (1, 4)), (0, 1, 32, 2.75))
    next_gain = jnp.clip(1.0 + 0.1 * jax.random.normal(keys[12], (D,), jnp.float32), 0.5, 1.5).astype(jnp.bfloat16)
    w_next_query = gaussian(keys[13], (D, QW), D ** -0.5, 0.125, ((0, 32), (1, 4)))
    w_next_kv = gaussian(keys[14], (D, 2, KVW), D ** -0.5, 0.125, ((0, 32), (2, 4)))
    tenant = touch_ends(jax.random.randint(keys[15], (REQ,), 0, TENANTS), jax.random.fold_in(keys[15], 1), 0, TENANTS - 1).astype(jnp.int32)
    guide_scale = jnp.clip(jnp.exp(jax.random.uniform(keys[16], (TENANTS,), jnp.float32, math.log(1.5), math.log(6.0))), 1.5, 6.0)
    return dict(hidden=hidden, lengths=lengths, kv_cache=kv_cache, attn_gain=attn_gain, w_query=w_query, w_key_value=w_key_value, w_out=w_out, mlp_gain=mlp_gain, w_gate_up=w_gate_up, w_down=w_down, final_gain=final_gain, w_head=w_head, next_gain=next_gain, w_next_query=w_next_query, w_next_kv=w_next_kv, tenant=tenant, guide_scale=guide_scale)


EPSILON = 1e-05
ROPE_BASE = 500000.0
NEGATIVE = -1e+30

def rotate(vectors, position):
    half_width = vectors.shape[-1] // 2
    frequency = ROPE_BASE ** (-2.0 * jnp.arange(half_width, dtype=jnp.float32) / vectors.shape[-1])
    angles = position.astype(jnp.float32)[:, None] * frequency[None, :]
    angles = angles.reshape((angles.shape[0],) + (1,) * (vectors.ndim - 2) + (half_width,))
    cosine = jnp.cos(angles)
    sines = jnp.sin(angles)
    first_half = vectors[..., :half_width]
    second_half = vectors[..., half_width:]
    return jnp.concatenate([first_half * cosine - second_half * sines, second_half * cosine + first_half * sines], axis=-1)

def norm_scale(values):
    return lax.rsqrt(lax.optimization_barrier(jnp.mean(values * values, axis=-1, keepdims=True)) + EPSILON)

def group_pass(x_rows, length, cache_block, attn_gain, w_query, w_key_value, w_out, mlp_gain, w_gate_up, w_down, final_gain, w_head, next_gain, w_next_query, w_next_kv):
    requests = x_rows.shape[0]
    group_size = HEADS // KVH
    x_float = x_rows.astype(jnp.float32)
    scaling = norm_scale(x_float)
    normed = (x_float * attn_gain.astype(jnp.float32)).astype(jnp.bfloat16)
    query = scaling * jnp.dot(normed, w_query, preferred_element_type=jnp.float32)
    key_value = scaling * jnp.dot(normed, w_key_value.reshape(D, 2 * KVW), preferred_element_type=jnp.float32)
    query = rotate(query.reshape(requests, KVH, group_size, HD), length).astype(jnp.bfloat16)
    new_key = rotate(key_value[:, :KVW].reshape(requests, KVH, HD), length).astype(jnp.bfloat16)
    new_value = key_value[:, KVW:].reshape(requests, KVH, HD).astype(jnp.bfloat16)
    cache_keys = cache_block[:, 0].reshape(requests, MAXLEN, KVH, HD)
    cache_values = cache_block[:, 1].reshape(requests, MAXLEN, KVH, HD)
    inv_scale = HD ** (-0.5)
    scores = jnp.einsum('bhgd,bshd->bhgs', query.astype(jnp.float32), cache_keys.astype(jnp.float32)) * inv_scale
    own_score = jnp.einsum('bhgd,bhd->bhg', query.astype(jnp.float32), new_key.astype(jnp.float32)) * inv_scale
    usable = (jnp.arange(MAXLEN, dtype=jnp.int32)[None, :] < length[:, None])[:, None, None, :]
    masked = jnp.where(usable, scores, NEGATIVE)
    best = jnp.maximum(lax.optimization_barrier(jnp.max(masked, axis=-1)), own_score)
    exp_terms = jnp.where(usable, jnp.exp(masked - best[..., None]), 0.0)
    own_exp = jnp.exp(own_score - best)
    norm_sum = lax.optimization_barrier(jnp.sum(exp_terms, axis=-1)) + own_exp
    rounded = lax.optimization_barrier(exp_terms.astype(jnp.bfloat16)).astype(jnp.float32)
    own_rounded = lax.optimization_barrier(own_exp.astype(jnp.bfloat16)).astype(jnp.float32)
    weighted = jnp.einsum('bhgs,bshd->bhgd', rounded, cache_values.astype(jnp.float32))
    weighted = weighted + own_rounded[..., None] * new_value.astype(jnp.float32)[:, :, None, :]
    attended = (weighted / norm_sum[..., None]).reshape(requests, QW).astype(jnp.bfloat16)
    residual_one = (x_float + jnp.dot(attended, w_out, preferred_element_type=jnp.float32)).astype(jnp.bfloat16)
    one_float = residual_one.astype(jnp.float32)
    mlp_scale = norm_scale(one_float)
    mlp_input = (one_float * mlp_gain.astype(jnp.float32)).astype(jnp.bfloat16)
    gate_up = jnp.dot(mlp_input, w_gate_up.reshape(D, 2 * FF), preferred_element_type=jnp.float32)
    activation = (jax.nn.silu(mlp_scale * gate_up[:, :FF]) * (mlp_scale * gate_up[:, FF:])).astype(jnp.bfloat16)
    residual_two = (one_float + jnp.dot(activation, w_down, preferred_element_type=jnp.float32)).astype(jnp.bfloat16)
    two_float = residual_two.astype(jnp.float32)
    out_scale = norm_scale(two_float)
    head_input = (two_float * final_gain.astype(jnp.float32)).astype(jnp.bfloat16)
    next_input = (two_float * next_gain.astype(jnp.float32)).astype(jnp.bfloat16)
    group_logits = out_scale * jnp.dot(head_input, w_head, preferred_element_type=jnp.float32)
    next_query = (out_scale * jnp.dot(next_input, w_next_query, preferred_element_type=jnp.float32)).astype(jnp.bfloat16)
    next_pairs = (out_scale * jnp.dot(next_input, w_next_kv.reshape(D, 2 * KVW), preferred_element_type=jnp.float32)).astype(jnp.bfloat16)
    return (group_logits, next_query, next_pairs.reshape(requests, 2, KVW))

def reference(hidden, lengths, kv_cache, attn_gain, w_query, w_key_value, w_out, mlp_gain, w_gate_up, w_down, final_gain, w_head, next_gain, w_next_query, w_next_kv, tenant, guide_scale):
    results = []
    for which in range(2):
        results.append(group_pass(hidden[which], lengths[which], kv_cache[which], attn_gain, w_query, w_key_value, w_out, mlp_gain, w_gate_up, w_down, final_gain, w_head, next_gain, w_next_query, w_next_kv))
    guidance = lax.optimization_barrier(jnp.sum(jnp.where(tenant[:, None] == jnp.arange(TENANTS, dtype=jnp.int32)[None, :], guide_scale[None, :], 0.0), axis=1))
    conditional = results[0][0]
    unconditional = results[1][0]
    guided_logits = unconditional + guidance[:, None] * (conditional - unconditional)
    next_query = jnp.stack([results[0][1], results[1][1]])
    next_key_value = jnp.stack([results[0][2], results[1][2]])
    return (guided_logits, next_query, next_key_value)
```

```python
import jax
import jax.numpy as jnp
from jax import lax
from jax.sharding import PartitionSpec as P

D = 2048
HEADS = 32
KVH = 8
HD = 64
TENANTS = 4
LANES = 128

EPSILON = 1e-05
ROPE_BASE = 500000.0
NEGATIVE = -1e30

F32 = jnp.float32
BF16 = jnp.bfloat16


def exchange(x, axis):
    return lax.all_to_all(x, axis, 0, 0, tiled=True)


def partner_2(x, axis, apart):
    return lax.ppermute(x, axis, [(i, i ^ 1 << apart) for i in range(lax.axis_size(axis))])


def rotate(vectors, position):
    half_width = vectors.shape[-1] // 2
    frequency = ROPE_BASE ** (-2.0 * jnp.arange(half_width, dtype=F32) / vectors.shape[-1])
    angles = position.astype(F32)[:, None] * frequency[None, :]
    angles = angles.reshape((angles.shape[0],) + (1,) * (vectors.ndim - 2) + (half_width,))
    cosine = jnp.cos(angles)
    sines = jnp.sin(angles)
    first_half = vectors[..., :half_width]
    second_half = vectors[..., half_width:]
    return jnp.concatenate(
        [first_half * cosine - second_half * sines, second_half * cosine + first_half * sines],
        axis=-1,
    )


def squares(values):
    return jnp.sum(values * values, axis=1)


def split(values, pieces):
    out = []
    rest = values
    for _ in range(pieces):
        piece = rest.astype(BF16)
        out.append(piece)
        rest = rest - piece.astype(F32)
    return out


def as_row(values):
    return jnp.pad(values, (0, LANES - values.shape[0]))[None, :]


def tiles(x):
    rows, width = x.shape
    return x.reshape(rows, width // LANES, LANES).transpose(1, 0, 2).reshape(-1, LANES)


def untiles(x, rows):
    return x.reshape(-1, rows, LANES).transpose(1, 0, 2).reshape(rows, -1)


def local(
    hidden,
    lengths,
    kv_cache,
    attn_gain,
    w_query,
    w_key_value,
    w_out,
    mlp_gain,
    w_gate_up,
    w_down,
    final_gain,
    w_head,
    next_gain,
    w_next_query,
    w_next_kv,
    tenant,
    guide_scale,
):
    x_rows = hidden[0]
    length = lengths[0]
    cache_block = kv_cache[0]
    requests = x_rows.shape[0]
    local_width = x_rows.shape[1]
    group_size = HEADS // KVH
    heads_here = w_key_value.shape[2] // HD
    peers = lax.axis_size("row")
    me = lax.axis_index("row")
    x_float = x_rows.astype(F32)
    normed = (x_float * attn_gain.astype(F32)).astype(BF16)
    query_part = jnp.dot(normed, w_query, preferred_element_type=F32)
    pair_part = jnp.dot(normed, w_key_value.reshape(local_width, -1), preferred_element_type=F32)
    own_part = (
        pair_part.astype(BF16)
        .reshape(requests, 2, heads_here, HD)
        .transpose(0, 2, 1, 3)
        .reshape(peers, 1, 2 * HD)
    )
    query_rows = tiles(query_part.astype(BF16))
    side = [as_row(piece) for piece in split(squares(x_float), 2)]
    shared = jnp.concatenate(side + [jnp.zeros((5, LANES), BF16)], axis=0)
    payload = jnp.concatenate(
        [
            jnp.broadcast_to(query_rows[None], (peers,) + query_rows.shape),
            own_part,
            jnp.broadcast_to(shared[None], (peers,) + shared.shape),
        ],
        axis=1,
    )
    total = jnp.sum(exchange(payload, "row").astype(F32), axis=0)
    depth = query_rows.shape[0]
    first_squares = total[depth + 1, :requests] + total[depth + 2, :requests]
    scaling = lax.rsqrt(first_squares / D + EPSILON)
    query = rotate(
        (scaling[:, None] * untiles(total[:depth], requests)).reshape(
            requests, heads_here, group_size, HD
        ),
        length,
    ).astype(BF16)
    own_request = me // heads_here
    own_head = me % heads_here
    own_pair = total[depth] * lax.dynamic_index_in_dim(scaling, own_request, 0, False)
    own_length = lax.dynamic_index_in_dim(length, own_request, 0, True)
    new_key = rotate(own_pair[None, :HD], own_length).astype(BF16)[0]
    new_value = own_pair[HD:].astype(BF16)
    cache_span = cache_block.shape[2]
    cache_keys = cache_block[:, 0].reshape(requests, cache_span, heads_here, HD)
    cache_values = cache_block[:, 1].reshape(requests, cache_span, heads_here, HD)
    inv_scale = HD ** (-0.5)
    scores = jnp.einsum("bhgd,bshd->bhgs", query, cache_keys, preferred_element_type=F32) * inv_scale
    positions = me * cache_span + jnp.arange(cache_span, dtype=jnp.int32)
    usable = (positions[None, :] < length[:, None])[:, None, None, :]
    mine_here = (
        (jnp.arange(requests) == own_request)[:, None] & (jnp.arange(heads_here) == own_head)[None, :]
    )[:, :, None]
    own_score = (
        jnp.sum(query.astype(F32) * new_key.astype(F32)[None, None, None, :], axis=-1) * inv_scale
    )
    masked = jnp.where(usable, scores, NEGATIVE)
    own_masked = jnp.where(mine_here, own_score, NEGATIVE)
    best = jnp.maximum(jnp.max(masked, axis=-1), own_masked)
    exp_terms = jnp.where(usable, jnp.exp(masked - best[..., None]), 0.0)
    own_exp = jnp.where(mine_here, jnp.exp(own_masked - best), 0.0)
    norm = jnp.sum(exp_terms, axis=-1) + own_exp
    weighted = jnp.einsum(
        "bhgs,bshd->bhgd", exp_terms.astype(BF16), cache_values, preferred_element_type=F32
    )
    weighted = weighted + own_exp.astype(BF16).astype(F32)[..., None] * new_value.astype(F32)
    average = weighted / jnp.where(norm > 0.0, norm, 1.0)[..., None]
    average_rows = tiles(average.reshape(requests, -1).astype(BF16))
    flat_heads = requests * heads_here * group_size
    side = [piece[None, :] for piece in split(best.reshape(flat_heads), 3)]
    side += [piece[None, :] for piece in split(norm.reshape(flat_heads), 2)]
    partial = jnp.concatenate([average_rows] + side + [jnp.zeros((3, LANES), BF16)], axis=0)
    parts = exchange(jnp.broadcast_to(partial[None], (peers,) + partial.shape), "row").astype(F32)
    bests = parts[:, depth] + (parts[:, depth + 1] + parts[:, depth + 2])
    norms = parts[:, depth + 3] + parts[:, depth + 4]
    factor = norms * jnp.exp(bests - jnp.max(bests, axis=0))
    factor = factor / jnp.sum(factor, axis=0)
    factor = jnp.repeat(factor.reshape(peers, requests, -1), HD, axis=2)
    factor = factor.reshape(peers, requests, -1, LANES).transpose(0, 2, 1, 3).reshape(peers, depth, LANES)
    attended = untiles(jnp.sum(parts[:, :depth] * factor, axis=0), requests).astype(BF16)
    out_part = jnp.dot(attended, w_out, preferred_element_type=F32)
    sides = lax.axis_size("col")
    out_sum = jnp.sum(
        exchange(jnp.broadcast_to(out_part[None], (sides,) + out_part.shape), "col"), axis=0
    )
    residual_one = (x_float + out_sum).astype(BF16)
    one_float = residual_one.astype(F32)
    mlp_input = (one_float * mlp_gain.astype(F32)).astype(BF16)
    gate_part = jnp.dot(
        mlp_input, w_gate_up.reshape(local_width, -1), preferred_element_type=F32
    ).astype(BF16)
    unit = w_gate_up.shape[2] // peers
    gate_rows = (
        gate_part.reshape(requests, 2, peers, unit)
        .transpose(2, 0, 1, 3)
        .reshape(peers, requests, 2 * unit)
    )
    side = jnp.concatenate(
        [as_row(piece) for piece in split(squares(one_float), 2)] + [jnp.zeros((6, LANES), BF16)],
        axis=0,
    )
    payload = jnp.concatenate(
        [gate_rows, jnp.broadcast_to(side[None], (peers,) + side.shape)], axis=1
    )
    total = jnp.sum(exchange(payload, "row").astype(F32), axis=0)
    second_squares = total[requests, :requests] + total[requests + 1, :requests]
    mlp_scale = lax.rsqrt(second_squares / D + EPSILON)[:, None]
    activation = (
        jax.nn.silu(mlp_scale * total[:requests, :unit]) * (mlp_scale * total[:requests, unit:])
    ).astype(BF16)
    units = exchange(jnp.broadcast_to(activation[None], (peers,) + activation.shape), "row")
    down_part = jnp.dot(
        units.transpose(1, 0, 2).reshape(requests, -1), w_down, preferred_element_type=F32
    )
    down_sum = jnp.sum(
        exchange(jnp.broadcast_to(down_part[None], (sides,) + down_part.shape), "col"), axis=0
    )
    residual_two = (one_float + down_sum).astype(BF16)
    guide_side = lax.axis_index("guide")
    other_two = partner_2(residual_two, "guide", 0)
    two_float = residual_two.astype(F32)
    groups = jnp.stack(
        [
            jnp.where(guide_side == 0, residual_two, other_two),
            jnp.where(guide_side == 0, other_two, residual_two),
        ]
    ).astype(F32)
    half_rows = requests // 2
    mine = lax.dynamic_slice_in_dim(groups, guide_side * half_rows, half_rows, 1)
    head_input = (mine * final_gain.astype(F32)).astype(BF16).reshape(requests, local_width)
    next_input = (two_float * next_gain.astype(F32)).astype(BF16)
    next_query_part = jnp.dot(next_input, w_next_query, preferred_element_type=F32)
    next_pair_part = jnp.dot(
        next_input, w_next_kv.reshape(local_width, -1), preferred_element_type=F32
    )
    query_width = next_query_part.shape[1]
    next_rows = tiles(
        jnp.concatenate([next_query_part, next_pair_part], axis=1).astype(BF16)
    ).reshape(peers, -1, LANES)
    chunk = next_rows.shape[1]
    both_squares = jnp.sum(groups * groups, axis=2).reshape(-1)
    side = jnp.concatenate(
        [as_row(piece) for piece in split(both_squares, 2)] + [jnp.zeros((6 - chunk, LANES), BF16)],
        axis=0,
    )
    payload = jnp.concatenate([next_rows, jnp.broadcast_to(side[None], (peers,) + side.shape)], axis=1)
    total = jnp.sum(exchange(payload, "row").astype(F32), axis=0)
    third_squares = (total[chunk] + total[chunk + 1])[: 2 * requests].reshape(2, requests)
    out_scale = lax.rsqrt(third_squares / D + EPSILON)
    guidance = jnp.sum(
        jnp.where(
            tenant[:, None] == jnp.arange(TENANTS, dtype=jnp.int32)[None, :],
            guide_scale[None, :],
            0.0,
        ),
        axis=1,
    )
    weights = jnp.stack([guidance, 1.0 - guidance]) * out_scale
    weights = lax.dynamic_slice_in_dim(weights, guide_side * half_rows, half_rows, 1)
    head_part = jnp.dot(head_input, w_head, preferred_element_type=F32)
    guided_part = (
        weights[0][:, None] * head_part[:half_rows] + weights[1][:, None] * head_part[half_rows:]
    ).astype(BF16)
    vocabulary = guided_part.shape[1]
    share = vocabulary // peers
    window = (share + 2 * LANES - 2) // LANES * LANES
    starts = [share * k // LANES * LANES for k in range(peers)]
    guided_part = jnp.pad(guided_part, ((0, 0), (0, max(0, starts[-1] + window - vocabulary))))
    pieces = jnp.stack([guided_part[:, start : start + window] for start in starts])
    next_piece = jnp.pad(total[:chunk].astype(BF16), ((0, half_rows - chunk), (0, 0)))
    payload = jnp.concatenate(
        [pieces, jnp.broadcast_to(next_piece[None], (peers,) + next_piece.shape)], axis=2
    )
    arrived = exchange(payload, "row")
    guided = jnp.sum(arrived[:, :, :window].astype(F32), axis=0)
    guided = lax.dynamic_slice_in_dim(guided, share * me % LANES, share, 1)
    next_all = untiles(arrived[:, :chunk, window:].reshape(-1, LANES), requests).astype(F32)
    own_scale = jnp.where(guide_side == 0, out_scale[0], out_scale[1])[:, None]
    next_all = (own_scale * next_all).astype(BF16)
    next_query = next_all[:, :query_width][None]
    next_key_value = next_all[:, query_width:].reshape(1, requests, 2, -1)
    return (guided, next_query, next_key_value)


def solution(mesh):
    placed = (
        P("guide", None, "row"),
        P("guide", None),
        P("guide", None, None, "row", "col"),
        P("row"),
        P("row", "col"),
        P("row", None, "col"),
        P("col", "row"),
        P("row"),
        P("row", None, "col"),
        P("col", "row"),
        P("row"),
        P("row", "col"),
        P("row"),
        P("row", "col"),
        P("row", None, "col"),
        P(),
        P(),
    )
    return jax.shard_map(
        local,
        mesh=mesh,
        in_specs=placed,
        out_specs=(
            P("guide", ("col", "row")),
            P("guide", None, "col"),
            P("guide", None, None, "col"),
        ),
        check_vma=False,
    )
```

```python
import functools

import jax
import jax.numpy as jnp
from jax import lax
from jax.experimental import pallas as pl
from jax.experimental.pallas import tpu as pltpu
from jax.sharding import PartitionSpec as P

D = 2048
HEADS = 32
KVH = 8
HD = 64
TENANTS = 4
LANES = 128
SUBLANES = 8

EPSILON = 1e-05
ROPE_BASE = 500000.0
NEGATIVE = -1e30

F32 = jnp.float32
BF16 = jnp.bfloat16
LANE_CONTRACT = (((1,), (1,)), ((), ()))


def exchange(x, axis):
    return lax.all_to_all(x, axis, 0, 0, tiled=True)


def partner_2(x, axis, apart):
    return lax.ppermute(x, axis, [(i, i ^ 1 << apart) for i in range(lax.axis_size(axis))])


def call(body, outs, *operands, scratch=(), scalars=0):
    specs = [pl.BlockSpec(memory_space=pltpu.SMEM)] * scalars
    specs += [pl.BlockSpec(memory_space=pltpu.VMEM)] * (len(operands) - scalars)
    out_specs = jax.tree.map(lambda _: pl.BlockSpec(memory_space=pltpu.VMEM), outs)
    return pl.pallas_call(
        body,
        out_shape=outs,
        in_specs=specs,
        out_specs=out_specs,
        scratch_shapes=list(scratch),
        compiler_params=pltpu.CompilerParams(vmem_limit_bytes=24 << 20),
    )(*operands)


def shape(dims, dtype):
    return jax.ShapeDtypeStruct(dims, dtype)


def index(dims, dim):
    return lax.broadcasted_iota(jnp.int32, dims, dim)


def low_lanes(rows):
    return index((rows, LANES), 1) < LANES // 2


def turned(x):
    return pltpu.roll(x, LANES // 2, 1)


def to_row(column, offset=0):
    n = column.shape[0]
    hit = index((n, LANES), 1) == index((n, LANES), 0) + offset
    return jnp.sum(jnp.where(hit, column, 0.0), axis=0, keepdims=True)


def to_column(row, n, offset=0):
    hit = index((n, LANES), 1) == index((n, LANES), 0) + offset
    return jnp.sum(jnp.where(hit, row, 0.0), axis=1, keepdims=True)


def halves(value):
    high = value.astype(BF16).astype(F32)
    return high, value - high


def block_of(rows):
    at = index((SUBLANES, LANES), 0)
    block = jnp.zeros((SUBLANES, LANES), F32)
    for k, row in enumerate(rows):
        block = jnp.where(at == k, row, block)
    return block


def summed(ref):
    total = ref[0].astype(F32)
    for k in range(1, ref.shape[0]):
        total = total + ref[k].astype(F32)
    return total


def norm_scale(total):
    return lax.rsqrt(total / D + EPSILON)


def spread(normed, which):
    width = normed.shape[1]
    dims = (width, 2 * width)
    pick = (index(dims, 1) == 2 * index(dims, 0) + which).astype(F32).astype(BF16)
    return jnp.dot(normed, pick, preferred_element_type=F32).astype(BF16)


def pair_dots(normed, pair_ref):
    weights = pair_ref[...]
    return [jnp.dot(spread(normed, w), weights, preferred_element_type=F32) for w in range(2)]


def start_kernel(x_ref, gain_ref, query_ref, pair_ref, out_ref):
    x = x_ref[...].astype(F32)
    requests = x.shape[0]
    normed = (x * gain_ref[...].astype(F32)).astype(BF16)
    query = jnp.dot(normed, query_ref[...], preferred_element_type=F32)
    tiles = query.shape[1] // LANES
    rows = jnp.concatenate(
        [query[:, j * LANES : (j + 1) * LANES] for j in range(tiles)], axis=0
    ).astype(BF16)
    keys, values = pair_dots(normed, pair_ref)
    low = low_lanes(requests)
    own = (jnp.where(low, keys, turned(values)), jnp.where(low, turned(keys), values))
    high_part, low_part = halves(to_row(jnp.sum(x * x, axis=1, keepdims=True)))
    depth = rows.shape[0]
    for peer in range(out_ref.shape[0]):
        request, head = divmod(peer, 2)
        side = block_of([own[head][request : request + 1], high_part, low_part])
        out_ref[peer, 0:depth] = rows
        out_ref[peer, depth : depth + SUBLANES] = side.astype(BF16)


def turn_pairs(x, cosine, sine):
    quarter = LANES // 4
    first = index(x.shape, 1) % (2 * quarter) < quarter
    other = jnp.where(first, pltpu.roll(x, 3 * quarter, 1), pltpu.roll(x, quarter, 1))
    return x * cosine + other * sine


def attention_kernel(me_ref, in_ref, cos_ref, sin_ref, length_ref, cache_ref, out_ref, q_ref, o_ref):
    me = me_ref[0]
    requests, _, span, _ = cache_ref.shape
    heads = SUBLANES
    total = summed(in_ref)
    depth = total.shape[0] - SUBLANES
    tiles = depth // requests
    scale_row = norm_scale(total[depth + 1 : depth + 2] + total[depth + 2 : depth + 3])
    scale = to_column(scale_row, requests)
    cosine = cos_ref[...]
    sine = sin_ref[...]
    low = low_lanes(requests)
    for j in range(tiles):
        tile = total[j * requests : (j + 1) * requests] * scale
        tile = turn_pairs(tile, cosine, sine).astype(BF16).astype(F32)
        if j < tiles // 2:
            pair = (jnp.where(low, tile, 0.0), jnp.where(low, turned(tile), 0.0))
        else:
            pair = (jnp.where(low, 0.0, turned(tile)), jnp.where(low, 0.0, tile))
        q_ref[pl.ds(2 * j, requests, stride=heads), :] = pair[0]
        q_ref[pl.ds(2 * j + 1, requests, stride=heads), :] = pair[1]
    own_request = me // 2
    own_head = me % 2
    pick = index((requests, LANES), 0) == own_request
    one_low = low_lanes(1)
    own_scale = jnp.sum(
        jnp.where(index((1, LANES), 1) == own_request, scale_row, 0.0), axis=1, keepdims=True
    )
    own_pair = total[depth : depth + 1] * own_scale
    own_cos = jnp.sum(jnp.where(pick, cosine, 0.0), axis=0, keepdims=True)
    own_sin = jnp.sum(jnp.where(pick, sine, 0.0), axis=0, keepdims=True)
    new_key = jnp.where(one_low, turn_pairs(own_pair, own_cos, own_sin), 0.0)
    new_value = jnp.where(one_low, 0.0, own_pair)
    new_key = jnp.where(own_head == 0, new_key, turned(new_key)).astype(BF16).astype(F32)
    new_value = jnp.where(own_head == 0, turned(new_value), new_value).astype(BF16).astype(F32)
    inv_scale = HD ** (-0.5)
    flat = requests * heads
    row = index((flat, 1), 0)
    mine = (row // heads == own_request) & (row % heads // (heads // 2) == own_head)
    own_score = jnp.sum(q_ref[...] * new_key, axis=1, keepdims=True) * inv_scale
    own_score = jnp.where(mine, own_score, NEGATIVE)
    scores = jnp.concatenate(
        [
            lax.dot_general(
                q_ref[b * heads : (b + 1) * heads, :].astype(BF16),
                cache_ref[b, 0],
                LANE_CONTRACT,
                preferred_element_type=F32,
            )
            for b in range(requests)
        ],
        axis=0,
    )
    usable = me * span + index((flat, span), 1) < length_ref[...]
    scores = jnp.where(usable, scores * inv_scale, NEGATIVE)
    best = jnp.maximum(jnp.max(scores, axis=1, keepdims=True), own_score)
    terms = jnp.where(usable, jnp.exp(scores - best), 0.0)
    own_term = jnp.where(mine, jnp.exp(own_score - best), 0.0)
    norm = jnp.sum(terms, axis=1, keepdims=True) + own_term
    weighted = jnp.concatenate(
        [
            jnp.dot(
                terms[b * heads : (b + 1) * heads].astype(BF16),
                cache_ref[b, 1],
                preferred_element_type=F32,
            )
            for b in range(requests)
        ],
        axis=0,
    )
    weighted = weighted + own_term.astype(BF16).astype(F32) * new_value
    o_ref[...] = weighted / jnp.where(norm > 0.0, norm, 1.0)
    average = []
    for i in range(heads // 2):
        first = o_ref[pl.ds(i, requests, stride=heads), :]
        second = o_ref[pl.ds(i + heads // 2, requests, stride=heads), :]
        average.append(jnp.where(low, first, second))
    lane = index((requests, LANES), 1)
    wide = []
    for value in (best, norm):
        o_ref[...] = jnp.broadcast_to(value, (flat, LANES))
        tile = jnp.zeros((requests, LANES), F32)
        for h in range(heads):
            tile = jnp.where(lane % heads == h, o_ref[pl.ds(h, requests, stride=heads), :], tile)
        wide.append(tile)
    best_high, rest = halves(wide[0])
    best_mid, best_low = halves(rest)
    norm_high, norm_low = halves(wide[1])
    side = jnp.zeros((requests, LANES), F32)
    for k, piece in enumerate((best_high, best_mid, best_low, norm_high, norm_low)):
        side = jnp.where(lane // heads == k, piece, side)
    block = jnp.concatenate(average + [side], axis=0).astype(BF16)
    for peer in range(out_ref.shape[0]):
        out_ref[peer] = block


def combine_kernel(in_ref, weight_ref, out_ref):
    peers, rows, _ = in_ref.shape
    heads = SUBLANES
    tiles = heads // 2
    requests = rows // (tiles + 1)
    depth = tiles * requests
    side = in_ref[:, depth:rows, :].astype(F32).reshape(peers * requests, LANES)

    def piece(k):
        return pltpu.roll(side, LANES - heads * k, 1) if k else side

    best = ((piece(0) + piece(1)) + piece(2)).reshape(peers, requests, LANES)
    norm = (piece(3) + piece(4)).reshape(peers, requests, LANES)
    factor = norm * jnp.exp(best - jnp.max(best, axis=0, keepdims=True))
    factor = factor / jnp.sum(factor, axis=0, keepdims=True)
    factor = factor.reshape(peers * requests, LANES)
    factor = jnp.where(index((peers * requests, LANES), 1) < heads, factor, 0.0)
    dims = (LANES, tiles * LANES)
    column = index(dims, 1)
    owner = column // LANES + tiles * (column % LANES // (LANES // 2))
    pick = (index(dims, 0) == owner).astype(F32).astype(BF16)
    high, low = halves(factor)
    factor = jnp.dot(high.astype(BF16), pick, preferred_element_type=F32) + jnp.dot(
        low.astype(BF16), pick, preferred_element_type=F32
    )
    sums = [jnp.zeros((requests, LANES), F32) for _ in range(tiles)]
    for peer in range(peers):
        for i in range(tiles):
            sums[i] = sums[i] + in_ref[peer, i * requests : (i + 1) * requests, :].astype(
                F32
            ) * factor[peer * requests : (peer + 1) * requests, i * LANES : (i + 1) * LANES]
    weights = weight_ref[...].astype(F32)
    take = low_lanes(weights.shape[0])
    total = jnp.zeros((requests, LANES), F32)
    for i in range(tiles):
        first = weights[:, i // 2 * LANES : (i // 2 + 1) * LANES]
        second = weights[:, (i // 2 + 2) * LANES : (i // 2 + 3) * LANES]
        if i % 2 == 0:
            tile = jnp.where(take, first, turned(second))
        else:
            tile = jnp.where(take, turned(first), second)
        tile = jnp.concatenate([tile, tile], axis=0).astype(BF16)
        total = total + lax.dot_general(
            sums[i].astype(BF16), tile, LANE_CONTRACT, preferred_element_type=F32
        )
    half = requests // 2
    packed = jnp.where(low_lanes(half), total[:half], total[half:])
    for side_at in range(out_ref.shape[0]):
        out_ref[side_at] = packed


def unpacked(packed):
    width = LANES // 2
    return jnp.concatenate([packed[:, :width], turned(packed)[:, :width]], axis=0)


def packed_squares(packed, offset=0):
    half = packed.shape[0]
    low = low_lanes(half)
    square = packed * packed
    first = jnp.sum(jnp.where(low, square, 0.0), axis=1, keepdims=True)
    second = jnp.sum(jnp.where(low, 0.0, square), axis=1, keepdims=True)
    return to_row(first, offset) + to_row(second, offset + half)


def gate_kernel(in_ref, x_ref, gain_ref, weight_ref, out_ref, one_ref):
    one = (x_ref[...] + summed(in_ref)).astype(BF16).astype(F32)
    one_ref[...] = one
    normed = unpacked(one * gain_ref[...]).astype(BF16)
    requests = normed.shape[0]
    both = jnp.dot(normed, weight_ref[...], preferred_element_type=F32)
    width = both.shape[1] // 2
    high_part, low_part = halves(packed_squares(one))
    side = block_of([high_part, low_part]).astype(BF16)
    low = low_lanes(requests)
    for t in range(width // LANES):
        gate = both[:, t * LANES : (t + 1) * LANES]
        up = both[:, width + t * LANES : width + (t + 1) * LANES]
        out_ref[2 * t, 0:requests] = jnp.where(low, gate, turned(up)).astype(BF16)
        out_ref[2 * t + 1, 0:requests] = jnp.where(low, turned(gate), up).astype(BF16)
        out_ref[2 * t, requests : requests + SUBLANES] = side
        out_ref[2 * t + 1, requests : requests + SUBLANES] = side


def activation_kernel(in_ref, out_ref):
    total = summed(in_ref)
    requests = total.shape[0] - SUBLANES
    scale_row = norm_scale(total[requests : requests + 1] + total[requests + 1 : requests + 2])
    both = total[:requests] * to_column(scale_row, requests)
    active = both / (1.0 + jnp.exp(-both)) * turned(both)
    half = requests // 2
    packed = jnp.where(low_lanes(half), active[:half], turned(active)[half:]).astype(BF16)
    for peer in range(out_ref.shape[0]):
        out_ref[peer] = packed


def down_kernel(in_ref, weight_ref, out_ref):
    peers, half, _ = in_ref.shape
    low = low_lanes(half)
    total = jnp.zeros((2 * half, LANES), F32)
    for t in range(peers // 2):
        first = in_ref[2 * t].astype(F32)
        second = in_ref[2 * t + 1].astype(F32)
        units = jnp.concatenate(
            [jnp.where(low, first, turned(second)), jnp.where(low, turned(first), second)], axis=0
        )
        tile = weight_ref[:, t * LANES : (t + 1) * LANES]
        tile = jnp.concatenate([tile, tile], axis=0)
        total = total + lax.dot_general(
            units.astype(BF16), tile, LANE_CONTRACT, preferred_element_type=F32
        )
    packed = jnp.where(low, total[:half], total[half:])
    for side_at in range(out_ref.shape[0]):
        out_ref[side_at] = packed


def next_kernel(
    guide_ref,
    own_ref,
    other_ref,
    final_ref,
    gain_ref,
    query_ref,
    pair_ref,
    out_ref,
    head_ref,
):
    guide = guide_ref[0]
    own = own_ref[...].astype(F32)
    other = other_ref[...].astype(F32)
    half = own.shape[0]
    normed = unpacked(own * gain_ref[...]).astype(BF16)
    query = jnp.dot(normed, query_ref[...], preferred_element_type=F32)
    tiles = [query[:, j * LANES : (j + 1) * LANES] for j in range(query.shape[1] // LANES)]
    tiles += pair_dots(normed, pair_ref)
    first = jnp.where(guide == 0, own, other)
    second = jnp.where(guide == 0, other, own)
    high_part, low_part = halves(packed_squares(first) + packed_squares(second, 2 * half))
    side = block_of([high_part, low_part])
    zero = jnp.zeros((half, LANES), F32)
    for peer in range(out_ref.shape[0]):
        j, part = divmod(peer, 2)
        piece = tiles[j][part * half : (part + 1) * half] if j < len(tiles) else zero
        out_ref[peer] = jnp.concatenate([piece, side], axis=0).astype(BF16)
    width = LANES // 2
    both = []
    for group in (first, second):
        group = group * final_ref[...]
        both.append(jnp.where(guide == 0, group, turned(group))[:, :width])
    head_ref[...] = jnp.concatenate(both, axis=0).astype(BF16)


def guided_kernel(spot_ref, in_ref, guidance_ref, head_ref, out_ref, *, starts, window):
    me = spot_ref[0]
    guide = spot_ref[1]
    total = summed(in_ref)
    half = SUBLANES
    scale_row = norm_scale(total[half : half + 1] + total[half + 1 : half + 2])

    def scales(offset):
        hit = index((half, LANES), 1) == index((half, LANES), 0) + offset
        return jnp.sum(jnp.where(hit, scale_row, 0.0), axis=1, keepdims=True)

    guidance = guidance_ref[...]
    first = guidance * scales(guide * half)
    second = (1.0 - guidance) * scales(2 * half + guide * half)
    piece = (total[:half] * scales(2 * half * guide + me % 2 * half)).astype(BF16)
    vocabulary = head_ref.shape[1]
    for peer, start in enumerate(starts):
        stop = min(start + window, vocabulary)
        part = first * head_ref[0:half, start:stop] + second * head_ref[half : 2 * half, start:stop]
        if stop - start < window:
            out_ref[peer, :, window - LANES : window] = jnp.zeros((half, LANES), BF16)
        out_ref[peer, :, 0 : stop - start] = part.astype(BF16)
        out_ref[peer, :, window : window + LANES] = piece


def finish_kernel(spot_ref, in_ref, guided_ref, query_ref, pair_ref, total_ref, pairs_ref, *, window):
    shift = spot_ref[0]
    total = in_ref[0, :, 0:window].astype(F32)
    for peer in range(1, in_ref.shape[0]):
        total = total + in_ref[peer, :, 0:window].astype(F32)
    total = pltpu.roll(total, shift, 1)
    guided_ref[...] = total[:, : guided_ref.shape[1]]
    tiles = query_ref.shape[1] // LANES
    half = in_ref.shape[1]

    def tile(j):
        return jnp.concatenate(
            [in_ref[2 * j, :, window : window + LANES], in_ref[2 * j + 1, :, window : window + LANES]],
            axis=0,
        )

    for j in range(tiles):
        query_ref[:, j * LANES : (j + 1) * LANES] = tile(j)
    for which in range(2):
        pairs_ref[pl.ds(which, 2 * half, stride=2), :] = tile(tiles + which).astype(F32)
    pair_ref[...] = pairs_ref[...].astype(BF16)


def local(
    hidden,
    lengths,
    kv_cache,
    attn_gain,
    w_query,
    w_key_value,
    w_out,
    mlp_gain,
    w_gate_up,
    w_down,
    final_gain,
    w_head,
    next_gain,
    w_next_query,
    w_next_kv,
    tenant,
    guide_scale,
):
    x_rows = hidden[0]
    length = lengths[0]
    cache_block = kv_cache[0]
    requests, local_width = x_rows.shape
    half = requests // 2
    heads = (HEADS // KVH) * (w_key_value.shape[2] // HD)
    peers = lax.axis_size("row")
    sides = lax.axis_size("col")
    me = lax.axis_index("row").astype(jnp.int32)
    guide = lax.axis_index("guide").astype(jnp.int32)

    def doubled(gain):
        gain = gain.astype(F32)
        return jnp.concatenate([gain, gain])[None, :]

    query_width = w_query.shape[1]
    depth = query_width // LANES * requests
    payload = call(
        start_kernel,
        shape((peers, depth + SUBLANES, LANES), BF16),
        x_rows,
        attn_gain[None, :],
        w_query,
        w_key_value.reshape(2 * local_width, -1),
    )
    arrived = exchange(payload, "row")
    quarter = LANES // 4
    lane = jnp.arange(LANES)
    frequency = ROPE_BASE ** (-2.0 * (lane % quarter).astype(F32) / HD)
    angles = length.astype(F32)[:, None] * frequency[None, :]
    cosine = jnp.cos(angles)
    sine = jnp.where(lane % (2 * quarter) < quarter, -1.0, 1.0)[None, :] * jnp.sin(angles)
    flat = requests * heads
    partial = call(
        attention_kernel,
        shape((peers, depth + requests, LANES), BF16),
        me[None],
        arrived,
        cosine,
        sine,
        jnp.repeat(length, heads)[:, None],
        cache_block,
        scratch=[pltpu.VMEM((flat, LANES), F32), pltpu.VMEM((flat, LANES), F32)],
        scalars=1,
    )
    arrived = exchange(partial, "row")
    packed_sums = call(
        combine_kernel, shape((sides, half, LANES), F32), arrived, w_out.T
    )
    arrived = exchange(packed_sums, "col")
    x_packed = jnp.concatenate([x_rows[:half], x_rows[half:]], axis=1).astype(F32)
    payload, one_packed = call(
        gate_kernel,
        (shape((peers, requests + SUBLANES, LANES), BF16), shape((half, LANES), F32)),
        arrived,
        x_packed,
        doubled(mlp_gain),
        w_gate_up.reshape(local_width, -1),
    )
    arrived = exchange(payload, "row")
    active = call(activation_kernel, shape((peers, half, LANES), BF16), arrived)
    arrived = exchange(active, "row")
    packed_sums = call(down_kernel, shape((sides, half, LANES), F32), arrived, w_down.T)
    arrived = exchange(packed_sums, "col")
    residual_two = (one_packed + jnp.sum(arrived, axis=0)).astype(BF16)
    other_two = partner_2(residual_two, "guide", 0)
    payload, head_input = call(
        next_kernel,
        (shape((peers, 2 * SUBLANES, LANES), BF16), shape((requests, local_width), BF16)),
        guide[None],
        residual_two,
        other_two,
        doubled(final_gain),
        doubled(next_gain),
        w_next_query,
        w_next_kv.reshape(2 * local_width, -1),
        scalars=1,
    )
    arrived = exchange(payload, "row")
    head_part = jnp.dot(head_input, w_head, preferred_element_type=F32)
    guidance = jnp.sum(
        jnp.where(
            tenant[:, None] == jnp.arange(TENANTS, dtype=jnp.int32)[None, :],
            guide_scale[None, :],
            0.0,
        ),
        axis=1,
    )
    my_guidance = lax.dynamic_slice_in_dim(guidance, guide * half, half, 0)[:, None]
    vocabulary = w_head.shape[1]
    share = vocabulary // peers
    window = (share + 2 * LANES - 2) // LANES * LANES
    starts = [share * k // LANES * LANES for k in range(peers)]
    payload = call(
        functools.partial(guided_kernel, starts=starts, window=window),
        shape((peers, half, window + LANES), BF16),
        jnp.stack([me, guide]),
        arrived,
        my_guidance,
        head_part,
        scalars=1,
    )
    arrived = exchange(payload, "row")
    shift = (window - share * me % LANES) % window
    guided, next_query, next_pairs = call(
        functools.partial(finish_kernel, window=window),
        (
            shape((half, share), F32),
            shape((requests, query_width), BF16),
            shape((2 * requests, LANES), BF16),
        ),
        shift[None],
        arrived,
        scratch=[pltpu.VMEM((half, window), F32), pltpu.VMEM((2 * requests, LANES), F32)],
        scalars=1,
    )
    return (guided, next_query[None], next_pairs.reshape(1, requests, 2, LANES))


def solution(mesh):
    placed = (
        P("guide", None, "row"),
        P("guide", None),
        P("guide", None, None, "row", "col"),
        P("row"),
        P("row", "col"),
        P("row", None, "col"),
        P("col", "row"),
        P("row"),
        P("row", None, "col"),
        P("col", "row"),
        P("row"),
        P("row", "col"),
        P("row"),
        P("row", "col"),
        P("row", None, "col"),
        P(),
        P(),
    )
    return jax.shard_map(
        local,
        mesh=mesh,
        in_specs=placed,
        out_specs=(
            P("guide", ("col", "row")),
            P("guide", None, "col"),
            P("guide", None, None, "col"),
        ),
        check_vma=False,
    )
```

```python
import functools

import jax
import jax.numpy as jnp
from jax import lax
from jax.experimental import pallas as pl
from jax.experimental.pallas import tpu as pltpu
from jax.sharding import PartitionSpec as P

D = 2048
HEADS = 32
KVH = 8
HD = 64
TENANTS = 4
LANES = 128
SUBLANES = 8
LINES = 4

EPSILON = 1e-05
ROPE_BASE = 500000.0
NEGATIVE = -1e30

F32 = jnp.float32
BF16 = jnp.bfloat16
LANE_CONTRACT = (((1,), (1,)), ((), ()))


def exchange(x, axis):
    return lax.all_to_all(x, axis, 0, 0, tiled=True)


def partner_2(x, axis, apart):
    return lax.ppermute(x, axis, [(i, i ^ 1 << apart) for i in range(lax.axis_size(axis))])


def from_others(x, axis):
    n = lax.axis_size(axis)
    return [lax.ppermute(x, axis, [(i, (i + k) % n) for i in range(n)]) for k in range(1, n)]


def call(body, outs, *operands, scratch=(), scalars=0):
    specs = [pl.BlockSpec(memory_space=pltpu.SMEM)] * scalars
    specs += [pl.BlockSpec(memory_space=pltpu.VMEM)] * (len(operands) - scalars)
    out_specs = jax.tree.map(lambda _: pl.BlockSpec(memory_space=pltpu.VMEM), outs)
    return pl.pallas_call(
        body,
        out_shape=outs,
        in_specs=specs,
        out_specs=out_specs,
        scratch_shapes=list(scratch),
        compiler_params=pltpu.CompilerParams(vmem_limit_bytes=24 << 20),
    )(*operands)


def shape(dims, dtype):
    return jax.ShapeDtypeStruct(dims, dtype)


def index(dims, dim):
    return lax.broadcasted_iota(jnp.int32, dims, dim)


def low_lanes(rows):
    return index((rows, LANES), 1) < LANES // 2


def turned(x):
    return pltpu.roll(x, LANES // 2, 1)


def to_row(column, offset=0):
    n = column.shape[0]
    hit = index((n, LANES), 1) == index((n, LANES), 0) + offset
    return jnp.sum(jnp.where(hit, column, 0.0), axis=0, keepdims=True)


def to_column(row, n, offset=0):
    hit = index((n, LANES), 1) == index((n, LANES), 0) + offset
    return jnp.sum(jnp.where(hit, row, 0.0), axis=1, keepdims=True)


def halves(value):
    high = value.astype(BF16).astype(F32)
    return high, value - high


def block_of(rows):
    at = index((SUBLANES, LANES), 0)
    block = jnp.zeros((SUBLANES, LANES), F32)
    for k, row in enumerate(rows):
        block = jnp.where(at == k, row, block)
    return block


def summed(ref):
    total = ref[0].astype(F32)
    for k in range(1, ref.shape[0]):
        total = total + ref[k].astype(F32)
    return total


def norm_scale(total):
    return lax.rsqrt(total / D + EPSILON)


def spread(normed, which):
    width = normed.shape[1]
    dims = (width, 2 * width)
    pick = (index(dims, 1) == 2 * index(dims, 0) + which).astype(F32).astype(BF16)
    return jnp.dot(normed, pick, preferred_element_type=F32).astype(BF16)


def pair_dots(normed, pair_ref):
    weights = pair_ref[...]
    return [jnp.dot(spread(normed, w), weights, preferred_element_type=F32) for w in range(2)]


def start_kernel(
    x_hbm, gain_hbm, query_hbm, pair_hbm, out_ref, x_ref, gain_ref, query_ref, pair_ref, sems
):
    sources = (x_hbm, gain_hbm, query_hbm, pair_hbm)
    targets = (x_ref, gain_ref, query_ref, pair_ref)
    copies = [
        pltpu.make_async_copy(source, target, sems.at[k])
        for k, (source, target) in enumerate(zip(sources, targets))
    ]
    for copy in copies:
        copy.start()
    for copy in copies:
        copy.wait()
    x = x_ref[...].astype(F32)
    requests = x.shape[0]
    normed = (x * gain_ref[...].astype(F32)).astype(BF16)
    query = jnp.dot(normed, query_ref[...], preferred_element_type=F32)
    keys, values = pair_dots(normed, pair_ref)
    low = low_lanes(requests)
    own = (jnp.where(low, keys, turned(values)), jnp.where(low, turned(keys), values))
    high_part, low_part = halves(to_row(jnp.sum(x * x, axis=1, keepdims=True)))
    half = requests // 2
    upper = index((half, LANES), 0) < half // 2
    variants = []
    for parity in range(2):
        pieces = []
        for tile in range(query.shape[1] // LANES):
            first = query[:half, tile * LANES : (tile + 1) * LANES]
            second = query[half:, tile * LANES : (tile + 1) * LANES]
            if parity:
                first = pltpu.roll(first, half // 2, 0)
                second = pltpu.roll(second, half // 2, 0)
            pieces.append(jnp.where(upper, first, second))
        variants.append(jnp.concatenate(pieces, axis=0).astype(BF16))
    depth = variants[0].shape[0]
    line = out_ref.shape[0] // LINES
    for peer in range(out_ref.shape[0]):
        column, place = divmod(peer, line)
        quarter = column % 2 if column < 2 else 3 - column % 2
        request = quarter * (requests // 4) + place // 2
        side = block_of([own[place % 2][request : request + 1], high_part, low_part])
        out_ref[peer, 0:depth] = variants[column % 2]
        out_ref[peer, depth : depth + SUBLANES] = side.astype(BF16)


def turn_pairs(x, cosine, sine):
    quarter = LANES // 4
    first = index(x.shape, 1) % (2 * quarter) < quarter
    other = jnp.where(first, pltpu.roll(x, 3 * quarter, 1), pltpu.roll(x, quarter, 1))
    return x * cosine + other * sine


def attention_kernel(
    me_ref,
    in_ref,
    cos_ref,
    sin_ref,
    length_ref,
    own_a_ref,
    own_b_ref,
    other_a_ref,
    other_b_ref,
    out_ref,
    q_ref,
    o_ref,
):
    share, _, span, _ = own_a_ref.shape
    heads = SUBLANES
    requests = 2 * share
    line = in_ref.shape[0] // LINES
    column = me_ref[0] // line
    place = me_ref[0] % line
    parity = column % 2
    total = summed(in_ref)
    depth = total.shape[0] - SUBLANES
    scale_row = norm_scale(total[depth + 1 : depth + 2] + total[depth + 2 : depth + 3])
    lane = index((requests, LANES), 1)
    row = index((requests, LANES), 0)
    wanted = jnp.where(row < share, parity * share + row, (2 - parity) * share + row)
    scale = jnp.sum(jnp.where(lane == wanted, scale_row, 0.0), axis=1, keepdims=True)
    cosine = cos_ref[...]
    sine = sin_ref[...]
    low = low_lanes(requests)
    tiles = depth // requests
    for j in range(tiles):
        tile = total[j * requests : (j + 1) * requests] * scale
        tile = turn_pairs(tile, cosine, sine).astype(BF16).astype(F32)
        other = turned(tile)
        if j < tiles // 2:
            even, odd = jnp.where(low, tile, 0.0), jnp.where(low, other, 0.0)
        else:
            even, odd = jnp.where(low, 0.0, other), jnp.where(low, 0.0, tile)
        q_ref[pl.ds(2 * j, requests, stride=heads), :] = even
        q_ref[pl.ds(2 * j + 1, requests, stride=heads), :] = odd
    own_request = column // 2 * share + place // 2
    own_head = place % 2
    one_low = low_lanes(1)
    pick = row == own_request
    own_scale = jnp.sum(jnp.where(pick[:, :1], scale, 0.0), axis=0, keepdims=True)
    own_pair = total[depth : depth + 1] * own_scale
    own_cos = jnp.sum(jnp.where(pick, cosine, 0.0), axis=0, keepdims=True)
    own_sin = jnp.sum(jnp.where(pick, sine, 0.0), axis=0, keepdims=True)
    new_key = jnp.where(one_low, turn_pairs(own_pair, own_cos, own_sin), 0.0)
    new_value = jnp.where(one_low, 0.0, own_pair)
    new_key = jnp.where(own_head == 0, new_key, turned(new_key)).astype(BF16).astype(F32)
    new_value = jnp.where(own_head == 0, turned(new_value), new_value).astype(BF16).astype(F32)
    inv_scale = HD ** (-0.5)
    flat = requests * heads
    flat_row = index((flat, 1), 0)
    mine = (flat_row // heads == own_request) & (flat_row % heads // (heads // 2) == own_head)
    own_score = jnp.sum(q_ref[...] * new_key, axis=1, keepdims=True) * inv_scale
    own_score = jnp.where(mine, own_score, NEGATIVE)
    near = column + 1 - 2 * parity
    far = lax.rem(column + LINES - 1 + 2 * parity, LINES)
    origins = (
        jnp.broadcast_to(column, (flat, 1)),
        jnp.where(flat_row < flat // 2, near, far),
    )
    best = own_score
    scored = []
    for block, (first, second) in enumerate(((own_a_ref, own_b_ref), (other_a_ref, other_b_ref))):
        scores = jnp.concatenate(
            [
                lax.dot_general(
                    q_ref[b * heads : (b + 1) * heads, :].astype(BF16),
                    (first if b < share else second)[b % share, 0],
                    LANE_CONTRACT,
                    preferred_element_type=F32,
                )
                for b in range(requests)
            ],
            axis=0,
        )
        position = (origins[block] * line + place) * span + index((flat, span), 1)
        usable = position < length_ref[...]
        scores = jnp.where(usable, scores * inv_scale, NEGATIVE)
        best = jnp.maximum(best, jnp.max(scores, axis=1, keepdims=True))
        scored.append((scores, usable, first, second))
    own_term = jnp.where(mine, jnp.exp(own_score - best), 0.0)
    norm = own_term
    weighted = own_term.astype(BF16).astype(F32) * new_value
    for scores, usable, first, second in scored:
        terms = jnp.where(usable, jnp.exp(scores - best), 0.0)
        norm = norm + jnp.sum(terms, axis=1, keepdims=True)
        weighted = weighted + jnp.concatenate(
            [
                jnp.dot(
                    terms[b * heads : (b + 1) * heads].astype(BF16),
                    (first if b < share else second)[b % share, 1],
                    preferred_element_type=F32,
                )
                for b in range(requests)
            ],
            axis=0,
        )
    o_ref[...] = weighted / jnp.where(norm > 0.0, norm, 1.0)
    blocks = []
    for i in range(heads // 2):
        first = o_ref[pl.ds(i, requests, stride=heads), :]
        second = o_ref[pl.ds(i + heads // 2, requests, stride=heads), :]
        blocks.append(jnp.where(low, first, second))
    wide = []
    for value in (best, norm):
        o_ref[...] = jnp.broadcast_to(value, (flat, LANES))
        tile = jnp.zeros((requests, LANES), F32)
        for h in range(heads):
            tile = jnp.where(lane % heads == h, o_ref[pl.ds(h, requests, stride=heads), :], tile)
        wide.append(tile)
    best_high, rest = halves(wide[0])
    best_mid, best_low = halves(rest)
    norm_high, norm_low = halves(wide[1])
    side = jnp.zeros((requests, LANES), F32)
    for k, piece in enumerate((best_high, best_mid, best_low, norm_high, norm_low)):
        side = jnp.where(lane // heads == k, piece, side)
    block = jnp.concatenate(blocks + [side], axis=0).astype(BF16)
    for peer in range(out_ref.shape[0]):
        out_ref[peer] = block


def combine_kernel(in_ref, weight_ref, out_ref):
    peers, rows, _ = in_ref.shape
    heads = SUBLANES
    half = SUBLANES
    tiles = heads // 2
    line = peers // LINES
    depth = rows - half
    flat = peers * half
    side = in_ref[:, depth:rows, :].astype(F32).reshape(flat, LANES)

    def piece(k):
        return pltpu.roll(side, LANES - heads * k, 1) if k else side

    def over_peers(reduce, value):
        return reduce(reduce(value, axis=2, keepdims=True), axis=0, keepdims=True)

    dims = (LINES // 2, 2, line, half, LANES)
    best = ((piece(0) + piece(1)) + piece(2)).reshape(dims)
    norm = (piece(3) + piece(4)).reshape(dims)
    factor = norm * jnp.exp(best - over_peers(jnp.max, best))
    factor = factor / over_peers(jnp.sum, factor)
    factor = factor.reshape(flat, LANES)
    factor = jnp.where(index((flat, LANES), 1) < heads, factor, 0.0)
    dims = (LANES, tiles * LANES)
    column = index(dims, 1)
    owner = column // LANES + tiles * (column % LANES // (LANES // 2))
    pick = (index(dims, 0) == owner).astype(F32).astype(BF16)
    high, rest = halves(factor)
    factor = jnp.dot(high.astype(BF16), pick, preferred_element_type=F32) + jnp.dot(
        rest.astype(BF16), pick, preferred_element_type=F32
    )
    weights = weight_ref[...].astype(F32)
    take = low_lanes(weights.shape[0])
    result = jnp.zeros((2 * half, LANES), F32)
    for i in range(tiles):
        averaged = [jnp.zeros((half, LANES), F32) for _ in range(2)]
        for peer in range(peers):
            parity = peer // line % 2
            averaged[parity] = averaged[parity] + in_ref[
                peer, i * half : (i + 1) * half, :
            ].astype(F32) * factor[peer * half : (peer + 1) * half, i * LANES : (i + 1) * LANES]
        first = weights[:, i // 2 * LANES : (i // 2 + 1) * LANES]
        second = weights[:, (i // 2 + 2) * LANES : (i // 2 + 3) * LANES]
        if i % 2 == 0:
            tile = jnp.where(take, first, turned(second))
        else:
            tile = jnp.where(take, turned(first), second)
        tile = jnp.concatenate([tile, tile], axis=0).astype(BF16)
        result = result + lax.dot_general(
            jnp.concatenate(averaged, axis=0).astype(BF16),
            tile,
            LANE_CONTRACT,
            preferred_element_type=F32,
        )
    outer = result[:half]
    inner = pltpu.roll(result[half:], half // 2, 0)
    upper = index((half, LANES), 0) < half // 2
    out_ref[...] = jnp.where(
        low_lanes(half), jnp.where(upper, outer, inner), jnp.where(upper, inner, outer)
    )


def unpacked(packed):
    width = LANES // 2
    return jnp.concatenate([packed[:, :width], turned(packed)[:, :width]], axis=0)


def packed_squares(packed, offset=0):
    half = packed.shape[0]
    low = low_lanes(half)
    square = packed * packed
    first = jnp.sum(jnp.where(low, square, 0.0), axis=1, keepdims=True)
    second = jnp.sum(jnp.where(low, 0.0, square), axis=1, keepdims=True)
    return to_row(first, offset) + to_row(second, offset + half)


def gate_kernel(own_ref, a_ref, b_ref, c_ref, x_ref, gain_ref, weight_ref, out_ref, one_ref):
    parts = (own_ref[...] + a_ref[...]) + (b_ref[...] + c_ref[...])
    one = (x_ref[...] + parts).astype(BF16).astype(F32)
    one_ref[...] = one
    normed = unpacked(one * gain_ref[...]).astype(BF16)
    requests = normed.shape[0]
    both = jnp.dot(normed, weight_ref[...], preferred_element_type=F32)
    width = both.shape[1] // 2
    high_part, low_part = halves(packed_squares(one))
    side = block_of([high_part, low_part]).astype(BF16)
    low = low_lanes(requests)
    for t in range(width // LANES):
        gate = both[:, t * LANES : (t + 1) * LANES]
        up = both[:, width + t * LANES : width + (t + 1) * LANES]
        out_ref[2 * t, 0:requests] = jnp.where(low, gate, turned(up)).astype(BF16)
        out_ref[2 * t + 1, 0:requests] = jnp.where(low, turned(gate), up).astype(BF16)
        out_ref[2 * t, requests : requests + SUBLANES] = side
        out_ref[2 * t + 1, requests : requests + SUBLANES] = side


def activation_kernel(in_ref, out_ref):
    total = summed(in_ref)
    requests = total.shape[0] - SUBLANES
    scale_row = norm_scale(total[requests : requests + 1] + total[requests + 1 : requests + 2])
    both = total[:requests] * to_column(scale_row, requests)
    active = both / (1.0 + jnp.exp(-both)) * turned(both)
    half = requests // 2
    packed = jnp.where(low_lanes(half), active[:half], turned(active)[half:]).astype(BF16)
    for peer in range(out_ref.shape[0]):
        out_ref[peer] = packed


def down_kernel(in_ref, weight_ref, out_ref):
    peers, half, _ = in_ref.shape
    low = low_lanes(half)
    total = jnp.zeros((2 * half, LANES), F32)
    for t in range(peers // 2):
        first = in_ref[2 * t].astype(F32)
        second = in_ref[2 * t + 1].astype(F32)
        units = jnp.concatenate(
            [jnp.where(low, first, turned(second)), jnp.where(low, turned(first), second)], axis=0
        )
        tile = weight_ref[:, t * LANES : (t + 1) * LANES]
        tile = jnp.concatenate([tile, tile], axis=0)
        total = total + lax.dot_general(
            units.astype(BF16), tile, LANE_CONTRACT, preferred_element_type=F32
        )
    out_ref[...] = jnp.where(low, total[:half], total[half:])


def next_kernel(
    guide_ref,
    own_ref,
    other_ref,
    final_ref,
    gain_ref,
    query_ref,
    pair_ref,
    out_ref,
    head_ref,
):
    guide = guide_ref[0]
    own = own_ref[...].astype(F32)
    other = other_ref[...].astype(F32)
    half = own.shape[0]
    normed = unpacked(own * gain_ref[...]).astype(BF16)
    query = jnp.dot(normed, query_ref[...], preferred_element_type=F32)
    tiles = [query[:, j * LANES : (j + 1) * LANES] for j in range(query.shape[1] // LANES)]
    tiles += pair_dots(normed, pair_ref)
    first = jnp.where(guide == 0, own, other)
    second = jnp.where(guide == 0, other, own)
    high_part, low_part = halves(packed_squares(first) + packed_squares(second, 2 * half))
    side = block_of([high_part, low_part])
    zero = jnp.zeros((half, LANES), F32)
    for peer in range(out_ref.shape[0]):
        j, part = divmod(peer, 2)
        piece = tiles[j][part * half : (part + 1) * half] if j < len(tiles) else zero
        out_ref[peer] = jnp.concatenate([piece, side], axis=0).astype(BF16)
    width = LANES // 2
    both = []
    for group in (first, second):
        group = group * final_ref[...]
        both.append(jnp.where(guide == 0, group, turned(group))[:, :width])
    head_ref[...] = jnp.concatenate(both, axis=0).astype(BF16)


def guided_kernel(spot_ref, in_ref, guidance_ref, head_ref, out_ref, *, starts, window):
    me = spot_ref[0]
    guide = spot_ref[1]
    total = summed(in_ref)
    half = SUBLANES
    scale_row = norm_scale(total[half : half + 1] + total[half + 1 : half + 2])

    def scales(offset):
        hit = index((half, LANES), 1) == index((half, LANES), 0) + offset
        return jnp.sum(jnp.where(hit, scale_row, 0.0), axis=1, keepdims=True)

    guidance = guidance_ref[...]
    first = guidance * scales(guide * half)
    second = (1.0 - guidance) * scales(2 * half + guide * half)
    piece = (total[:half] * scales(2 * half * guide + me % 2 * half)).astype(BF16)
    vocabulary = head_ref.shape[1]
    for peer, start in enumerate(starts):
        stop = min(start + window, vocabulary)
        part = first * head_ref[0:half, start:stop] + second * head_ref[half : 2 * half, start:stop]
        if stop - start < window:
            out_ref[peer, :, window - LANES : window] = jnp.zeros((half, LANES), BF16)
        out_ref[peer, :, 0 : stop - start] = part.astype(BF16)
        out_ref[peer, :, window : window + LANES] = piece


def finish_kernel(spot_ref, in_ref, guided_ref, query_ref, pair_ref, total_ref, pairs_ref, *, window):
    shift = spot_ref[0]
    total = in_ref[0, :, 0:window].astype(F32)
    for peer in range(1, in_ref.shape[0]):
        total = total + in_ref[peer, :, 0:window].astype(F32)
    total = pltpu.roll(total, shift, 1)
    guided_ref[...] = total[:, : guided_ref.shape[1]]
    tiles = query_ref.shape[1] // LANES
    half = in_ref.shape[1]

    def tile(j):
        return jnp.concatenate(
            [in_ref[2 * j, :, window : window + LANES], in_ref[2 * j + 1, :, window : window + LANES]],
            axis=0,
        )

    for j in range(tiles):
        query_ref[:, j * LANES : (j + 1) * LANES] = tile(j)
    for which in range(2):
        pairs_ref[pl.ds(which, 2 * half, stride=2), :] = tile(tiles + which).astype(F32)
    pair_ref[...] = pairs_ref[...].astype(BF16)


def local(
    hidden,
    lengths,
    kv_cache,
    attn_gain,
    w_query,
    w_key_value,
    w_out,
    mlp_gain,
    w_gate_up,
    w_down,
    final_gain,
    w_head,
    next_gain,
    w_next_query,
    w_next_kv,
    tenant,
    guide_scale,
):
    x_rows = hidden[0]
    length = lengths[0]
    cache_block = kv_cache[0]
    requests, local_width = x_rows.shape
    half = requests // 2
    peers = lax.axis_size("row")
    me = lax.axis_index("row").astype(jnp.int32)
    guide = lax.axis_index("guide").astype(jnp.int32)

    def doubled(gain):
        gain = gain.astype(F32)
        return jnp.concatenate([gain, gain])[None, :]

    query_width = w_query.shape[1]
    line = peers // LINES
    share = requests // 4
    column = me // line
    parity = column % 2

    def quarter_of(source, which):
        return lax.dynamic_slice_in_dim(source, which * share, share, 0)

    def between(block, partner):
        pairs = [(i, partner(i // line) % LINES * line + i % line) for i in range(peers)]
        return lax.ppermute(block, "row", pairs)

    sent = [quarter_of(cache_block, k) for k in (1 - parity, 2 + parity)]
    x_first, sent, cache_later = lax.optimization_barrier((x_rows, sent, cache_block))
    caches = [quarter_of(cache_later, k) for k in (parity, 3 - parity)] + [
        between(sent[0], lambda k: k + 1 - 2 * (k % 2)),
        between(sent[1], lambda k: k - 1 + 2 * (k % 2)),
    ]
    depth = query_width // LANES * half
    operands = [
        pltpu.with_memory_space_constraint(operand, pltpu.HBM)
        for operand in (
            x_first,
            attn_gain[None, :],
            w_query,
            w_key_value.reshape(2 * local_width, -1),
        )
    ]
    payload = pl.pallas_call(
        start_kernel,
        out_shape=shape((peers, depth + SUBLANES, LANES), BF16),
        in_specs=[pl.BlockSpec(memory_space=pltpu.HBM)] * len(operands),
        out_specs=pl.BlockSpec(memory_space=pltpu.VMEM),
        scratch_shapes=[pltpu.VMEM(operand.shape, operand.dtype) for operand in operands]
        + [pltpu.SemaphoreType.DMA((len(operands),))],
        compiler_params=pltpu.CompilerParams(vmem_limit_bytes=24 << 20),
    )(*operands)
    arrived = exchange(payload, "row")
    my_lengths = jnp.where(
        parity == 0,
        jnp.concatenate([length[:share], length[3 * share :]]),
        length[share : 3 * share],
    )
    quarter = LANES // 4
    lane = jnp.arange(LANES)
    frequency = ROPE_BASE ** (-2.0 * (lane % quarter).astype(F32) / HD)
    angles = my_lengths.astype(F32)[:, None] * frequency[None, :]
    cosine = jnp.cos(angles)
    sine = jnp.where(lane % (2 * quarter) < quarter, -1.0, 1.0)[None, :] * jnp.sin(angles)
    flat = half * SUBLANES
    partial = call(
        attention_kernel,
        shape((peers, depth + SUBLANES, LANES), BF16),
        me[None],
        arrived,
        cosine,
        sine,
        jnp.repeat(my_lengths, SUBLANES)[:, None],
        *caches,
        scratch=[
            pltpu.VMEM((flat, LANES), F32),
            pltpu.VMEM((flat, LANES), F32),
        ],
        scalars=1,
    )
    arrived = exchange(partial, "row")
    out_part = call(combine_kernel, shape((half, LANES), F32), arrived, w_out.T)
    x_packed = jnp.concatenate([x_rows[:half], x_rows[half:]], axis=1).astype(F32)
    payload, one_packed = call(
        gate_kernel,
        (shape((peers, requests + SUBLANES, LANES), BF16), shape((half, LANES), F32)),
        out_part,
        *from_others(out_part, "col"),
        x_packed,
        doubled(mlp_gain),
        w_gate_up.reshape(local_width, -1),
    )
    arrived = exchange(payload, "row")
    active = call(activation_kernel, shape((peers, half, LANES), BF16), arrived)
    arrived = exchange(active, "row")
    down_part = call(down_kernel, shape((half, LANES), F32), arrived, w_down.T)
    a, b, c = from_others(down_part, "col")
    residual_two = (one_packed + ((down_part + a) + (b + c))).astype(BF16)
    other_two = partner_2(residual_two, "guide", 0)
    payload, head_input = call(
        next_kernel,
        (shape((peers, 2 * SUBLANES, LANES), BF16), shape((requests, local_width), BF16)),
        guide[None],
        residual_two,
        other_two,
        doubled(final_gain),
        doubled(next_gain),
        w_next_query,
        w_next_kv.reshape(2 * local_width, -1),
        scalars=1,
    )
    arrived = exchange(payload, "row")
    head_part = jnp.dot(head_input, w_head, preferred_element_type=F32)
    guidance = jnp.sum(
        jnp.where(
            tenant[:, None] == jnp.arange(TENANTS, dtype=jnp.int32)[None, :],
            guide_scale[None, :],
            0.0,
        ),
        axis=1,
    )
    my_guidance = lax.dynamic_slice_in_dim(guidance, guide * half, half, 0)[:, None]
    vocabulary = w_head.shape[1]
    part = vocabulary // peers
    window = (part + 2 * LANES - 2) // LANES * LANES
    starts = [part * k // LANES * LANES for k in range(peers)]
    payload = call(
        functools.partial(guided_kernel, starts=starts, window=window),
        shape((peers, half, window + LANES), BF16),
        jnp.stack([me, guide]),
        arrived,
        my_guidance,
        head_part,
        scalars=1,
    )
    arrived = exchange(payload, "row")
    shift = (window - part * me % LANES) % window
    guided, next_query, next_pairs = call(
        functools.partial(finish_kernel, window=window),
        (
            shape((half, part), F32),
            shape((requests, query_width), BF16),
            shape((2 * requests, LANES), BF16),
        ),
        shift[None],
        arrived,
        scratch=[pltpu.VMEM((half, window), F32), pltpu.VMEM((2 * requests, LANES), F32)],
        scalars=1,
    )
    return (guided, next_query[None], next_pairs.reshape(1, requests, 2, LANES))


def solution(mesh):
    placed = (
        P("guide", None, "row"),
        P("guide", None),
        P("guide", None, None, "row", "col"),
        P("row"),
        P("row", "col"),
        P("row", None, "col"),
        P("col", "row"),
        P("row"),
        P("row", None, "col"),
        P("col", "row"),
        P("row"),
        P("row", "col"),
        P("row"),
        P("row", "col"),
        P("row", None, "col"),
        P(),
        P(),
    )
    return jax.shard_map(
        local,
        mesh=mesh,
        in_specs=placed,
        out_specs=(
            P("guide", ("col", "row")),
            P("guide", None, "col"),
            P("guide", None, None, "col"),
        ),
        check_vma=False,
    )
```

```python
import functools

import jax
import jax.numpy as jnp
from jax import lax
from jax.experimental import pallas as pl
from jax.experimental.pallas import tpu as pltpu
from jax.sharding import PartitionSpec as P

D = 2048
HEADS = 32
KVH = 8
HD = 64
TENANTS = 4
LANES = 128
SUBLANES = 8
LINES = 4

EPSILON = 1e-05
ROPE_BASE = 500000.0
NEGATIVE = -1e30

F32 = jnp.float32
BF16 = jnp.bfloat16
LANE_CONTRACT = (((1,), (1,)), ((), ()))


def exchange(x, axis):
    return lax.all_to_all(x, axis, 0, 0, tiled=True)


def partner_2(x, axis, apart):
    return lax.ppermute(x, axis, [(i, i ^ 1 << apart) for i in range(lax.axis_size(axis))])


def from_others(x, axis):
    n = lax.axis_size(axis)
    return [lax.ppermute(x, axis, [(i, (i + k) % n) for i in range(n)]) for k in range(1, n)]


def call(body, outs, *operands, scratch=(), scalars=0):
    specs = [pl.BlockSpec(memory_space=pltpu.SMEM)] * scalars
    specs += [pl.BlockSpec(memory_space=pltpu.VMEM)] * (len(operands) - scalars)
    out_specs = jax.tree.map(lambda _: pl.BlockSpec(memory_space=pltpu.VMEM), outs)
    return pl.pallas_call(
        body,
        out_shape=outs,
        in_specs=specs,
        out_specs=out_specs,
        scratch_shapes=list(scratch),
        compiler_params=pltpu.CompilerParams(vmem_limit_bytes=24 << 20),
    )(*operands)


def shape(dims, dtype):
    return jax.ShapeDtypeStruct(dims, dtype)


def index(dims, dim):
    return lax.broadcasted_iota(jnp.int32, dims, dim)


def low_lanes(rows):
    return index((rows, LANES), 1) < LANES // 2


def turned(x):
    return pltpu.roll(x, LANES // 2, 1)


def to_row(column, offset=0):
    n = column.shape[0]
    hit = index((n, LANES), 1) == index((n, LANES), 0) + offset
    return jnp.sum(jnp.where(hit, column, 0.0), axis=0, keepdims=True)


def to_column(row, n, offset=0):
    hit = index((n, LANES), 1) == index((n, LANES), 0) + offset
    return jnp.sum(jnp.where(hit, row, 0.0), axis=1, keepdims=True)


def halves(value):
    high = value.astype(BF16).astype(F32)
    return high, value - high


def block_of(rows):
    at = index((SUBLANES, LANES), 0)
    block = jnp.zeros((SUBLANES, LANES), F32)
    for k, row in enumerate(rows):
        block = jnp.where(at == k, row, block)
    return block


def summed(ref):
    total = ref[0].astype(F32)
    for k in range(1, ref.shape[0]):
        total = total + ref[k].astype(F32)
    return total


def norm_scale(total):
    return lax.rsqrt(total / D + EPSILON)


def spread(normed, which):
    width = normed.shape[1]
    dims = (width, 2 * width)
    pick = (index(dims, 1) == 2 * index(dims, 0) + which).astype(F32).astype(BF16)
    return jnp.dot(normed, pick, preferred_element_type=F32).astype(BF16)


def pair_dots(normed, pair_ref):
    weights = pair_ref[...]
    return [jnp.dot(spread(normed, w), weights, preferred_element_type=F32) for w in range(2)]


def start_kernel(
    x_hbm, gain_hbm, query_hbm, pair_hbm, out_ref, x_ref, gain_ref, query_ref, pair_ref, sems
):
    sources = (x_hbm, gain_hbm, query_hbm, pair_hbm)
    targets = (x_ref, gain_ref, query_ref, pair_ref)
    copies = [
        pltpu.make_async_copy(source, target, sems.at[k])
        for k, (source, target) in enumerate(zip(sources, targets))
    ]
    for copy in copies:
        copy.start()
    for copy in copies:
        copy.wait()
    x = x_ref[...].astype(F32)
    requests = x.shape[0]
    normed = (x * gain_ref[...].astype(F32)).astype(BF16)
    query = jnp.dot(normed, query_ref[...], preferred_element_type=F32)
    keys, values = pair_dots(normed, pair_ref)
    low = low_lanes(requests)
    own = (jnp.where(low, keys, turned(values)), jnp.where(low, turned(keys), values))
    high_part, low_part = halves(to_row(jnp.sum(x * x, axis=1, keepdims=True)))
    half = requests // 2
    upper = index((half, LANES), 0) < half // 2
    variants = []
    for parity in range(2):
        pieces = []
        for tile in range(query.shape[1] // LANES):
            first = query[:half, tile * LANES : (tile + 1) * LANES]
            second = query[half:, tile * LANES : (tile + 1) * LANES]
            if parity:
                first = pltpu.roll(first, half // 2, 0)
                second = pltpu.roll(second, half // 2, 0)
            pieces.append(jnp.where(upper, first, second))
        variants.append(jnp.concatenate(pieces, axis=0).astype(BF16))
    depth = variants[0].shape[0]
    line = out_ref.shape[0] // LINES
    for peer in range(out_ref.shape[0]):
        column, place = divmod(peer, line)
        quarter = column % 2 if column < 2 else 3 - column % 2
        request = quarter * (requests // 4) + place // 2
        side = block_of([own[place % 2][request : request + 1], high_part, low_part])
        out_ref[peer, 0:depth] = variants[column % 2]
        out_ref[peer, depth : depth + SUBLANES] = side.astype(BF16)


def turn_pairs(x, cosine, sine):
    quarter = LANES // 4
    first = index(x.shape, 1) % (2 * quarter) < quarter
    other = jnp.where(first, pltpu.roll(x, 3 * quarter, 1), pltpu.roll(x, quarter, 1))
    return x * cosine + other * sine


def attention_kernel(
    me_ref,
    in_ref,
    cos_ref,
    sin_ref,
    length_ref,
    own_a_ref,
    own_b_ref,
    other_a_ref,
    other_b_ref,
    out_ref,
    q_ref,
    o_ref,
):
    share, _, span, _ = own_a_ref.shape
    heads = SUBLANES
    requests = 2 * share
    line = in_ref.shape[0] // LINES
    column = me_ref[0] // line
    place = me_ref[0] % line
    parity = column % 2
    total = summed(in_ref)
    depth = total.shape[0] - SUBLANES
    scale_row = norm_scale(total[depth + 1 : depth + 2] + total[depth + 2 : depth + 3])
    lane = index((requests, LANES), 1)
    row = index((requests, LANES), 0)
    wanted = jnp.where(row < share, parity * share + row, (2 - parity) * share + row)
    scale = jnp.sum(jnp.where(lane == wanted, scale_row, 0.0), axis=1, keepdims=True)
    cosine = cos_ref[...]
    sine = sin_ref[...]
    low = low_lanes(requests)
    tiles = depth // requests
    for j in range(tiles):
        tile = total[j * requests : (j + 1) * requests] * scale
        tile = turn_pairs(tile, cosine, sine).astype(BF16).astype(F32)
        other = turned(tile)
        if j < tiles // 2:
            even, odd = jnp.where(low, tile, 0.0), jnp.where(low, other, 0.0)
        else:
            even, odd = jnp.where(low, 0.0, other), jnp.where(low, 0.0, tile)
        q_ref[pl.ds(2 * j, requests, stride=heads), :] = even
        q_ref[pl.ds(2 * j + 1, requests, stride=heads), :] = odd
    own_request = column // 2 * share + place // 2
    own_head = place % 2
    one_low = low_lanes(1)
    pick = row == own_request
    own_scale = jnp.sum(jnp.where(pick[:, :1], scale, 0.0), axis=0, keepdims=True)
    own_pair = total[depth : depth + 1] * own_scale
    own_cos = jnp.sum(jnp.where(pick, cosine, 0.0), axis=0, keepdims=True)
    own_sin = jnp.sum(jnp.where(pick, sine, 0.0), axis=0, keepdims=True)
    new_key = jnp.where(one_low, turn_pairs(own_pair, own_cos, own_sin), 0.0)
    new_value = jnp.where(one_low, 0.0, own_pair)
    new_key = jnp.where(own_head == 0, new_key, turned(new_key)).astype(BF16).astype(F32)
    new_value = jnp.where(own_head == 0, turned(new_value), new_value).astype(BF16).astype(F32)
    inv_scale = HD ** (-0.5)
    flat = requests * heads
    flat_row = index((flat, 1), 0)
    mine = (flat_row // heads == own_request) & (flat_row % heads // (heads // 2) == own_head)
    own_score = jnp.sum(q_ref[...] * new_key, axis=1, keepdims=True) * inv_scale
    own_score = jnp.where(mine, own_score, NEGATIVE)
    near = column + 1 - 2 * parity
    far = lax.rem(column + LINES - 1 + 2 * parity, LINES)
    origins = (
        jnp.broadcast_to(column, (flat, 1)),
        jnp.where(flat_row < flat // 2, near, far),
    )
    best = own_score
    scored = []
    for block, (first, second) in enumerate(((own_a_ref, own_b_ref), (other_a_ref, other_b_ref))):
        scores = jnp.concatenate(
            [
                lax.dot_general(
                    q_ref[b * heads : (b + 1) * heads, :].astype(BF16),
                    (first if b < share else second)[b % share, 0],
                    LANE_CONTRACT,
                    preferred_element_type=F32,
                )
                for b in range(requests)
            ],
            axis=0,
        )
        position = (origins[block] * line + place) * span + index((flat, span), 1)
        usable = position < length_ref[...]
        scores = jnp.where(usable, scores * inv_scale, NEGATIVE)
        best = jnp.maximum(best, jnp.max(scores, axis=1, keepdims=True))
        scored.append((scores, usable, first, second))
    own_term = jnp.where(mine, jnp.exp(own_score - best), 0.0)
    norm = own_term
    weighted = own_term.astype(BF16).astype(F32) * new_value
    for scores, usable, first, second in scored:
        terms = jnp.where(usable, jnp.exp(scores - best), 0.0)
        norm = norm + jnp.sum(terms, axis=1, keepdims=True)
        weighted = weighted + jnp.concatenate(
            [
                jnp.dot(
                    terms[b * heads : (b + 1) * heads].astype(BF16),
                    (first if b < share else second)[b % share, 1],
                    preferred_element_type=F32,
                )
                for b in range(requests)
            ],
            axis=0,
        )
    o_ref[...] = weighted / jnp.where(norm > 0.0, norm, 1.0)
    blocks = []
    for i in range(heads // 2):
        first = o_ref[pl.ds(i, requests, stride=heads), :]
        second = o_ref[pl.ds(i + heads // 2, requests, stride=heads), :]
        blocks.append(jnp.where(low, first, second))
    wide = []
    for value in (best, norm):
        o_ref[...] = jnp.broadcast_to(value, (flat, LANES))
        tile = jnp.zeros((requests, LANES), F32)
        for h in range(heads):
            tile = jnp.where(lane % heads == h, o_ref[pl.ds(h, requests, stride=heads), :], tile)
        wide.append(tile)
    best_high, rest = halves(wide[0])
    best_mid, best_low = halves(rest)
    norm_high, norm_low = halves(wide[1])
    side = jnp.zeros((requests, LANES), F32)
    for k, piece in enumerate((best_high, best_mid, best_low, norm_high, norm_low)):
        side = jnp.where(lane // heads == k, piece, side)
    block = jnp.concatenate(blocks + [side], axis=0).astype(BF16)
    for peer in range(out_ref.shape[0]):
        out_ref[peer] = block


def combine_kernel(in_ref, weight_ref, out_ref):
    peers, rows, _ = in_ref.shape
    heads = SUBLANES
    half = SUBLANES
    tiles = heads // 2
    line = peers // LINES
    depth = rows - half
    flat = peers * half
    side = in_ref[:, depth:rows, :].astype(F32).reshape(flat, LANES)

    def piece(k):
        return pltpu.roll(side, LANES - heads * k, 1) if k else side

    def over_peers(reduce, value):
        return reduce(reduce(value, axis=2, keepdims=True), axis=0, keepdims=True)

    dims = (LINES // 2, 2, line, half, LANES)
    best = ((piece(0) + piece(1)) + piece(2)).reshape(dims)
    norm = (piece(3) + piece(4)).reshape(dims)
    factor = norm * jnp.exp(best - over_peers(jnp.max, best))
    factor = factor / over_peers(jnp.sum, factor)
    factor = factor.reshape(flat, LANES)
    factor = jnp.where(index((flat, LANES), 1) < heads, factor, 0.0)
    dims = (LANES, tiles * LANES)
    column = index(dims, 1)
    owner = column // LANES + tiles * (column % LANES // (LANES // 2))
    pick = (index(dims, 0) == owner).astype(F32).astype(BF16)
    high, rest = halves(factor)
    factor = jnp.dot(high.astype(BF16), pick, preferred_element_type=F32) + jnp.dot(
        rest.astype(BF16), pick, preferred_element_type=F32
    )
    weights = weight_ref[...].astype(F32)
    take = low_lanes(weights.shape[0])
    result = jnp.zeros((2 * half, LANES), F32)
    for i in range(tiles):
        averaged = [jnp.zeros((half, LANES), F32) for _ in range(2)]
        for peer in range(peers):
            parity = peer // line % 2
            averaged[parity] = averaged[parity] + in_ref[
                peer, i * half : (i + 1) * half, :
            ].astype(F32) * factor[peer * half : (peer + 1) * half, i * LANES : (i + 1) * LANES]
        first = weights[:, i // 2 * LANES : (i // 2 + 1) * LANES]
        second = weights[:, (i // 2 + 2) * LANES : (i // 2 + 3) * LANES]
        if i % 2 == 0:
            tile = jnp.where(take, first, turned(second))
        else:
            tile = jnp.where(take, turned(first), second)
        tile = jnp.concatenate([tile, tile], axis=0).astype(BF16)
        result = result + lax.dot_general(
            jnp.concatenate(averaged, axis=0).astype(BF16),
            tile,
            LANE_CONTRACT,
            preferred_element_type=F32,
        )
    outer = result[:half]
    inner = pltpu.roll(result[half:], half // 2, 0)
    upper = index((half, LANES), 0) < half // 2
    out_ref[...] = jnp.where(
        low_lanes(half), jnp.where(upper, outer, inner), jnp.where(upper, inner, outer)
    )


def unpacked(packed):
    width = LANES // 2
    return jnp.concatenate([packed[:, :width], turned(packed)[:, :width]], axis=0)


def packed_squares(packed, offset=0):
    half = packed.shape[0]
    low = low_lanes(half)
    square = packed * packed
    first = jnp.sum(jnp.where(low, square, 0.0), axis=1, keepdims=True)
    second = jnp.sum(jnp.where(low, 0.0, square), axis=1, keepdims=True)
    return to_row(first, offset) + to_row(second, offset + half)


def gate_kernel(own_ref, a_ref, b_ref, c_ref, x_ref, gain_ref, weight_ref, out_ref, one_ref):
    parts = (own_ref[...] + a_ref[...]) + (b_ref[...] + c_ref[...])
    one = (x_ref[...] + parts).astype(BF16).astype(F32)
    one_ref[...] = one
    normed = unpacked(one * gain_ref[...]).astype(BF16)
    requests = normed.shape[0]
    both = jnp.dot(normed, weight_ref[...], preferred_element_type=F32)
    width = both.shape[1] // 2
    high_part, low_part = halves(packed_squares(one))
    side = block_of([high_part, low_part]).astype(BF16)
    low = low_lanes(requests)
    for t in range(width // LANES):
        gate = both[:, t * LANES : (t + 1) * LANES]
        up = both[:, width + t * LANES : width + (t + 1) * LANES]
        out_ref[2 * t, 0:requests] = jnp.where(low, gate, turned(up)).astype(BF16)
        out_ref[2 * t + 1, 0:requests] = jnp.where(low, turned(gate), up).astype(BF16)
        out_ref[2 * t, requests : requests + SUBLANES] = side
        out_ref[2 * t + 1, requests : requests + SUBLANES] = side


def activation_kernel(in_ref, out_ref):
    total = summed(in_ref)
    requests = total.shape[0] - SUBLANES
    scale_row = norm_scale(total[requests : requests + 1] + total[requests + 1 : requests + 2])
    both = total[:requests] * to_column(scale_row, requests)
    active = both / (1.0 + jnp.exp(-both)) * turned(both)
    half = requests // 2
    packed = jnp.where(low_lanes(half), active[:half], turned(active)[half:]).astype(BF16)
    for peer in range(out_ref.shape[0]):
        out_ref[peer] = packed


def down_kernel(in_ref, weight_ref, out_ref):
    peers, half, _ = in_ref.shape
    low = low_lanes(half)
    total = jnp.zeros((2 * half, LANES), F32)
    for t in range(peers // 2):
        first = in_ref[2 * t].astype(F32)
        second = in_ref[2 * t + 1].astype(F32)
        units = jnp.concatenate(
            [jnp.where(low, first, turned(second)), jnp.where(low, turned(first), second)], axis=0
        )
        tile = weight_ref[:, t * LANES : (t + 1) * LANES]
        tile = jnp.concatenate([tile, tile], axis=0)
        total = total + lax.dot_general(
            units.astype(BF16), tile, LANE_CONTRACT, preferred_element_type=F32
        )
    out_ref[...] = jnp.where(low, total[:half], total[half:])


def next_kernel(
    guide_ref,
    own_ref,
    other_ref,
    final_ref,
    gain_ref,
    query_ref,
    pair_ref,
    out_ref,
    head_ref,
):
    guide = guide_ref[0]
    own = own_ref[...].astype(F32)
    other = other_ref[...].astype(F32)
    half = own.shape[0]
    normed = unpacked(own * gain_ref[...]).astype(BF16)
    query = jnp.dot(normed, query_ref[...], preferred_element_type=F32)
    tiles = [query[:, j * LANES : (j + 1) * LANES] for j in range(query.shape[1] // LANES)]
    tiles += pair_dots(normed, pair_ref)
    first = jnp.where(guide == 0, own, other)
    second = jnp.where(guide == 0, other, own)
    high_part, low_part = halves(packed_squares(first) + packed_squares(second, 2 * half))
    side = block_of([high_part, low_part])
    zero = jnp.zeros((half, LANES), F32)
    line = out_ref.shape[0] // LINES
    for peer in range(out_ref.shape[0]):
        j, part = divmod(peer // line // 2 * line + peer % line, 2)
        piece = tiles[j][part * half : (part + 1) * half] if j < len(tiles) else zero
        out_ref[peer] = jnp.concatenate([piece, side], axis=0).astype(BF16)
    width = LANES // 2
    both = []
    for group in (first, second):
        group = group * final_ref[...]
        both.append(jnp.where(guide == 0, group, turned(group))[:, :width])
    head_ref[...] = jnp.concatenate(both, axis=0).astype(BF16)


def windows_of(parity, starts):
    line = len(starts) // LINES
    return [start for peer, start in enumerate(starts) if peer // line % 2 == parity]


def window_rows(ref, wide_ref, rows, start, width):
    origin = start // LANES * LANES
    wide = wide_ref.shape[1]
    stop = min(origin + wide, ref.shape[1])
    value = ref[rows, origin:stop]
    if stop - origin < wide:
        wide_ref[...] = jnp.zeros(wide_ref.shape, F32)
        wide_ref[:, 0 : stop - origin] = value
        value = wide_ref[...]
    return pltpu.roll(value, (wide - start + origin) % wide, 1)[:, :width]


def share_kernel(spot_ref, head_ref, cond_ref, plain_ref, wide_ref, *, starts):
    parity = spot_ref[0]
    half = head_ref.shape[0] // 2
    width = cond_ref.shape[2]

    def write(sent):
        for slot, start in enumerate(windows_of(sent, starts)):
            for k, ref in enumerate((cond_ref, plain_ref)):
                rows = slice(k * half, (k + 1) * half)
                ref[slot] = window_rows(head_ref, wide_ref, rows, start, width).astype(BF16)

    pl.when(parity == 0)(lambda: write(1))
    pl.when(parity != 0)(lambda: write(0))


def guided_kernel(
    spot_ref, in_ref, guidance_ref, head_ref, cond_ref, plain_ref, out_ref, wide_ref, *, starts
):
    me = spot_ref[0]
    guide = spot_ref[1]
    parity = spot_ref[2]
    total = summed(in_ref)
    half = SUBLANES
    scale_row = norm_scale(total[half : half + 1] + total[half + 1 : half + 2])

    def scales(offset):
        hit = index((half, LANES), 1) == index((half, LANES), 0) + offset
        return jnp.sum(jnp.where(hit, scale_row, 0.0), axis=1, keepdims=True)

    guidance = guidance_ref[...]
    first = guidance * scales(guide * half)
    second = (1.0 - guidance) * scales(2 * half + guide * half)
    piece = (total[:half] * scales(2 * half * guide + me % 2 * half)).astype(BF16)
    width = cond_ref.shape[2]

    def write(kept):
        for slot, start in enumerate(windows_of(kept, starts)):
            cond = window_rows(head_ref, wide_ref, slice(0, half), start, width)
            plain = window_rows(head_ref, wide_ref, slice(half, 2 * half), start, width)
            cond = cond + cond_ref[slot].astype(F32)
            plain = plain + plain_ref[slot].astype(F32)
            out_ref[slot, :, 0:width] = (first * cond + second * plain).astype(BF16)
            out_ref[slot, :, width : width + LANES] = piece

    pl.when(parity == 0)(lambda: write(0))
    pl.when(parity != 0)(lambda: write(1))


def finish_kernel(in_ref, guided_ref, query_ref, pair_ref, pairs_ref):
    window = in_ref.shape[2] - LANES
    total = in_ref[0, :, 0:window].astype(F32)
    for peer in range(1, in_ref.shape[0]):
        total = total + in_ref[peer, :, 0:window].astype(F32)
    guided_ref[...] = total[:, : guided_ref.shape[1]]
    tiles = query_ref.shape[1] // LANES
    half = in_ref.shape[1]

    def tile(j):
        return jnp.concatenate(
            [in_ref[2 * j, :, window : window + LANES], in_ref[2 * j + 1, :, window : window + LANES]],
            axis=0,
        )

    for j in range(tiles):
        query_ref[:, j * LANES : (j + 1) * LANES] = tile(j)
    for which in range(2):
        pairs_ref[pl.ds(which, 2 * half, stride=2), :] = tile(tiles + which).astype(F32)
    pair_ref[...] = pairs_ref[...].astype(BF16)


def local(
    hidden,
    lengths,
    kv_cache,
    attn_gain,
    w_query,
    w_key_value,
    w_out,
    mlp_gain,
    w_gate_up,
    w_down,
    final_gain,
    w_head,
    next_gain,
    w_next_query,
    w_next_kv,
    tenant,
    guide_scale,
):
    x_rows = hidden[0]
    length = lengths[0]
    cache_block = kv_cache[0]
    requests, local_width = x_rows.shape
    half = requests // 2
    peers = lax.axis_size("row")
    me = lax.axis_index("row").astype(jnp.int32)
    guide = lax.axis_index("guide").astype(jnp.int32)

    def doubled(gain):
        gain = gain.astype(F32)
        return jnp.concatenate([gain, gain])[None, :]

    query_width = w_query.shape[1]
    line = peers // LINES
    share = requests // 4
    column = me // line
    parity = column % 2

    def quarter_of(source, which):
        return lax.dynamic_slice_in_dim(source, which * share, share, 0)

    def nearer(k):
        return k + 1 - 2 * (k % 2)

    def farther(k):
        return k - 1 + 2 * (k % 2)

    def between(block, partner):
        pairs = [(i, partner(i // line) % LINES * line + i % line) for i in range(peers)]
        return lax.ppermute(block, "row", pairs)

    sent = [quarter_of(cache_block, k) for k in (1 - parity, 2 + parity)]
    x_first, sent, cache_later = lax.optimization_barrier((x_rows, sent, cache_block))
    caches = [quarter_of(cache_later, k) for k in (parity, 3 - parity)] + [
        between(sent[0], nearer),
        between(sent[1], farther),
    ]
    depth = query_width // LANES * half
    operands = [
        pltpu.with_memory_space_constraint(operand, pltpu.HBM)
        for operand in (
            x_first,
            attn_gain[None, :],
            w_query,
            w_key_value.reshape(2 * local_width, -1),
        )
    ]
    payload = pl.pallas_call(
        start_kernel,
        out_shape=shape((peers, depth + SUBLANES, LANES), BF16),
        in_specs=[pl.BlockSpec(memory_space=pltpu.HBM)] * len(operands),
        out_specs=pl.BlockSpec(memory_space=pltpu.VMEM),
        scratch_shapes=[pltpu.VMEM(operand.shape, operand.dtype) for operand in operands]
        + [pltpu.SemaphoreType.DMA((len(operands),))],
        compiler_params=pltpu.CompilerParams(vmem_limit_bytes=24 << 20),
    )(*operands)
    arrived = exchange(payload, "row")
    my_lengths = jnp.where(
        parity == 0,
        jnp.concatenate([length[:share], length[3 * share :]]),
        length[share : 3 * share],
    )
    quarter = LANES // 4
    lane = jnp.arange(LANES)
    frequency = ROPE_BASE ** (-2.0 * (lane % quarter).astype(F32) / HD)
    angles = my_lengths.astype(F32)[:, None] * frequency[None, :]
    cosine = jnp.cos(angles)
    sine = jnp.where(lane % (2 * quarter) < quarter, -1.0, 1.0)[None, :] * jnp.sin(angles)
    flat = half * SUBLANES
    partial = call(
        attention_kernel,
        shape((peers, depth + SUBLANES, LANES), BF16),
        me[None],
        arrived,
        cosine,
        sine,
        jnp.repeat(my_lengths, SUBLANES)[:, None],
        *caches,
        scratch=[
            pltpu.VMEM((flat, LANES), F32),
            pltpu.VMEM((flat, LANES), F32),
        ],
        scalars=1,
    )
    arrived = exchange(partial, "row")
    out_part = call(combine_kernel, shape((half, LANES), F32), arrived, w_out.T)
    x_packed = jnp.concatenate([x_rows[:half], x_rows[half:]], axis=1).astype(F32)
    payload, one_packed = call(
        gate_kernel,
        (shape((peers, requests + SUBLANES, LANES), BF16), shape((half, LANES), F32)),
        out_part,
        *from_others(out_part, "col"),
        x_packed,
        doubled(mlp_gain),
        w_gate_up.reshape(local_width, -1),
    )
    arrived = exchange(payload, "row")
    active = call(activation_kernel, shape((peers, half, LANES), BF16), arrived)
    arrived = exchange(active, "row")
    down_part = call(down_kernel, shape((half, LANES), F32), arrived, w_down.T)
    a, b, c = from_others(down_part, "col")
    residual_two = (one_packed + ((down_part + a) + (b + c))).astype(BF16)
    other_two = partner_2(residual_two, "guide", 0)
    payload, head_input = call(
        next_kernel,
        (shape((peers, 2 * SUBLANES, LANES), BF16), shape((requests, local_width), BF16)),
        guide[None],
        residual_two,
        other_two,
        doubled(final_gain),
        doubled(next_gain),
        w_next_query,
        w_next_kv.reshape(2 * local_width, -1),
        scalars=1,
    )
    arrived = exchange(payload, "row")
    head_part = jnp.dot(head_input, w_head, preferred_element_type=F32)
    guidance = jnp.sum(
        jnp.where(
            tenant[:, None] == jnp.arange(TENANTS, dtype=jnp.int32)[None, :],
            guide_scale[None, :],
            0.0,
        ),
        axis=1,
    )
    my_guidance = lax.dynamic_slice_in_dim(guidance, guide * half, half, 0)[:, None]
    vocabulary = w_head.shape[1]
    part = vocabulary // peers
    width = (part + LANES - 1) // LANES * LANES
    starts = [part * k for k in range(peers)]
    wide = pltpu.VMEM((half, width + LANES), F32)
    members = peers // 2
    cond_sent, plain_sent = call(
        functools.partial(share_kernel, starts=starts),
        (shape((members, half, width), BF16), shape((members, half, width), BF16)),
        parity[None],
        head_part,
        scratch=[wide],
        scalars=1,
    )
    payload = call(
        functools.partial(guided_kernel, starts=starts),
        shape((members, half, width + LANES), BF16),
        jnp.stack([me, guide, parity]),
        arrived,
        my_guidance,
        head_part,
        between(cond_sent, nearer),
        between(plain_sent, farther),
        scratch=[wide],
        scalars=1,
    )
    groups = [[i for i in range(peers) if i // line % 2 == k] for k in range(2)]
    arrived = lax.all_to_all(payload, "row", 0, 0, axis_index_groups=groups, tiled=True)
    guided, next_query, next_pairs = call(
        finish_kernel,
        (
            shape((half, part), F32),
            shape((requests, query_width), BF16),
            shape((2 * requests, LANES), BF16),
        ),
        arrived,
        scratch=[pltpu.VMEM((2 * requests, LANES), F32)],
    )
    return (guided, next_query[None], next_pairs.reshape(1, requests, 2, LANES))


def solution(mesh):
    placed = (
        P("guide", None, "row"),
        P("guide", None),
        P("guide", None, None, "row", "col"),
        P("row"),
        P("row", "col"),
        P("row", None, "col"),
        P("col", "row"),
        P("row"),
        P("row", None, "col"),
        P("col", "row"),
        P("row"),
        P("row", "col"),
        P("row"),
        P("row", "col"),
        P("row", None, "col"),
        P(),
        P(),
    )
    return jax.shard_map(
        local,
        mesh=mesh,
        in_specs=placed,
        out_specs=(
            P("guide", ("col", "row")),
            P("guide", None, "col"),
            P("guide", None, None, "col"),
        ),
        check_vma=False,
    )
```

```python
import functools

import jax
import jax.numpy as jnp
from jax import lax
from jax.experimental import pallas as pl
from jax.experimental.pallas import tpu as pltpu
from jax.sharding import PartitionSpec as P

D = 2048
HEADS = 32
KVH = 8
HD = 64
TENANTS = 4
LANES = 128
SUBLANES = 8
LINES = 4

EPSILON = 1e-05
ROPE_BASE = 500000.0
NEGATIVE = -1e30

F32 = jnp.float32
BF16 = jnp.bfloat16
LANE_CONTRACT = (((1,), (1,)), ((), ()))


def exchange(x, axis):
    return lax.all_to_all(x, axis, 0, 0, tiled=True)


def partner_2(x, axis, apart):
    return lax.ppermute(x, axis, [(i, i ^ 1 << apart) for i in range(lax.axis_size(axis))])


def from_others(x, axis):
    n = lax.axis_size(axis)
    return [lax.ppermute(x, axis, [(i, (i + k) % n) for i in range(n)]) for k in range(1, n)]


def call(body, outs, *operands, scratch=(), scalars=0, in_hbm=0, limit=8 << 20):
    specs = [pl.BlockSpec(memory_space=pltpu.SMEM)] * scalars
    specs += [pl.BlockSpec(memory_space=pltpu.VMEM)] * (len(operands) - scalars - in_hbm)
    specs += [pl.BlockSpec(memory_space=pltpu.HBM)] * in_hbm
    out_specs = jax.tree.map(lambda _: pl.BlockSpec(memory_space=pltpu.VMEM), outs)
    return pl.pallas_call(
        body,
        out_shape=outs,
        in_specs=specs,
        out_specs=out_specs,
        scratch_shapes=list(scratch),
        compiler_params=pltpu.CompilerParams(vmem_limit_bytes=limit),
    )(*operands)


def shape(dims, dtype):
    return jax.ShapeDtypeStruct(dims, dtype)


def index(dims, dim):
    return lax.broadcasted_iota(jnp.int32, dims, dim)


def low_lanes(rows):
    return index((rows, LANES), 1) < LANES // 2


def turned(x):
    return pltpu.roll(x, LANES // 2, 1)


def to_row(column, offset=0):
    n = column.shape[0]
    hit = index((n, LANES), 1) == index((n, LANES), 0) + offset
    return jnp.sum(jnp.where(hit, column, 0.0), axis=0, keepdims=True)


def to_column(row, n, offset=0):
    hit = index((n, LANES), 1) == index((n, LANES), 0) + offset
    return jnp.sum(jnp.where(hit, row, 0.0), axis=1, keepdims=True)


def halves(value):
    high = value.astype(BF16).astype(F32)
    return high, value - high


def block_of(rows):
    at = index((SUBLANES, LANES), 0)
    block = jnp.zeros((SUBLANES, LANES), F32)
    for k, row in enumerate(rows):
        block = jnp.where(at == k, row, block)
    return block


def summed(ref):
    total = ref[0].astype(F32)
    for k in range(1, ref.shape[0]):
        total = total + ref[k].astype(F32)
    return total


def norm_scale(total):
    return lax.rsqrt(total / D + EPSILON)


def spread(normed, which):
    width = normed.shape[1]
    dims = (width, 2 * width)
    pick = (index(dims, 1) == 2 * index(dims, 0) + which).astype(F32).astype(BF16)
    return jnp.dot(normed, pick, preferred_element_type=F32).astype(BF16)


def pair_dots(normed, pair_ref):
    weights = pair_ref[...]
    return [jnp.dot(spread(normed, w), weights, preferred_element_type=F32) for w in range(2)]


def start_kernel(
    x_hbm, gain_hbm, query_hbm, pair_hbm, out_ref, x_ref, gain_ref, query_ref, pair_ref, sems
):
    sources = (x_hbm, gain_hbm, query_hbm, pair_hbm)
    targets = (x_ref, gain_ref, query_ref, pair_ref)
    copies = [
        pltpu.make_async_copy(source, target, sems.at[k])
        for k, (source, target) in enumerate(zip(sources, targets))
    ]
    for copy in copies:
        copy.start()
    for copy in copies:
        copy.wait()
    x = x_ref[...].astype(F32)
    requests = x.shape[0]
    normed = (x * gain_ref[...].astype(F32)).astype(BF16)
    query = jnp.dot(normed, query_ref[...], preferred_element_type=F32)
    keys, values = pair_dots(normed, pair_ref)
    low = low_lanes(requests)
    own = (jnp.where(low, keys, turned(values)), jnp.where(low, turned(keys), values))
    high_part, low_part = halves(to_row(jnp.sum(x * x, axis=1, keepdims=True)))
    half = requests // 2
    upper = index((half, LANES), 0) < half // 2
    variants = []
    for parity in range(2):
        pieces = []
        for tile in range(query.shape[1] // LANES):
            first = query[:half, tile * LANES : (tile + 1) * LANES]
            second = query[half:, tile * LANES : (tile + 1) * LANES]
            if parity:
                first = pltpu.roll(first, half // 2, 0)
                second = pltpu.roll(second, half // 2, 0)
            pieces.append(jnp.where(upper, first, second))
        variants.append(jnp.concatenate(pieces, axis=0).astype(BF16))
    depth = variants[0].shape[0]
    line = out_ref.shape[0] // LINES
    for peer in range(out_ref.shape[0]):
        column, place = divmod(peer, line)
        quarter = column % 2 if column < 2 else 3 - column % 2
        request = quarter * (requests // 4) + place // 2
        side = block_of([own[place % 2][request : request + 1], high_part, low_part])
        out_ref[peer, 0:depth] = variants[column % 2]
        out_ref[peer, depth : depth + SUBLANES] = side.astype(BF16)


def turn_pairs(x, cosine, sine):
    quarter = LANES // 4
    first = index(x.shape, 1) % (2 * quarter) < quarter
    other = jnp.where(first, pltpu.roll(x, 3 * quarter, 1), pltpu.roll(x, quarter, 1))
    return x * cosine + other * sine


def attention_kernel(
    me_ref,
    in_ref,
    cos_ref,
    sin_ref,
    length_ref,
    own_a_ref,
    own_b_ref,
    other_a_ref,
    other_b_ref,
    out_ref,
    q_ref,
    o_ref,
):
    share, _, span, _ = own_a_ref.shape
    heads = SUBLANES
    requests = 2 * share
    line = in_ref.shape[0] // LINES
    column = me_ref[0] // line
    place = me_ref[0] % line
    parity = column % 2
    total = summed(in_ref)
    depth = total.shape[0] - SUBLANES
    scale_row = norm_scale(total[depth + 1 : depth + 2] + total[depth + 2 : depth + 3])
    lane = index((requests, LANES), 1)
    row = index((requests, LANES), 0)
    wanted = jnp.where(row < share, parity * share + row, (2 - parity) * share + row)
    scale = jnp.sum(jnp.where(lane == wanted, scale_row, 0.0), axis=1, keepdims=True)
    cosine = cos_ref[...]
    sine = sin_ref[...]
    low = low_lanes(requests)
    tiles = depth // requests
    for j in range(tiles):
        tile = total[j * requests : (j + 1) * requests] * scale
        tile = turn_pairs(tile, cosine, sine).astype(BF16).astype(F32)
        other = turned(tile)
        if j < tiles // 2:
            even, odd = jnp.where(low, tile, 0.0), jnp.where(low, other, 0.0)
        else:
            even, odd = jnp.where(low, 0.0, other), jnp.where(low, 0.0, tile)
        q_ref[pl.ds(2 * j, requests, stride=heads), :] = even
        q_ref[pl.ds(2 * j + 1, requests, stride=heads), :] = odd
    own_request = column // 2 * share + place // 2
    own_head = place % 2
    one_low = low_lanes(1)
    pick = row == own_request
    own_scale = jnp.sum(jnp.where(pick[:, :1], scale, 0.0), axis=0, keepdims=True)
    own_pair = total[depth : depth + 1] * own_scale
    own_cos = jnp.sum(jnp.where(pick, cosine, 0.0), axis=0, keepdims=True)
    own_sin = jnp.sum(jnp.where(pick, sine, 0.0), axis=0, keepdims=True)
    new_key = jnp.where(one_low, turn_pairs(own_pair, own_cos, own_sin), 0.0)
    new_value = jnp.where(one_low, 0.0, own_pair)
    new_key = jnp.where(own_head == 0, new_key, turned(new_key)).astype(BF16).astype(F32)
    new_value = jnp.where(own_head == 0, turned(new_value), new_value).astype(BF16).astype(F32)
    inv_scale = HD ** (-0.5)
    flat = requests * heads
    flat_row = index((flat, 1), 0)
    mine = (flat_row // heads == own_request) & (flat_row % heads // (heads // 2) == own_head)
    own_score = jnp.sum(q_ref[...] * new_key, axis=1, keepdims=True) * inv_scale
    own_score = jnp.where(mine, own_score, NEGATIVE)
    near = column + 1 - 2 * parity
    far = lax.rem(column + LINES - 1 + 2 * parity, LINES)
    origins = (
        jnp.broadcast_to(column, (flat, 1)),
        jnp.where(flat_row < flat // 2, near, far),
    )
    best = own_score
    scored = []
    for block, (first, second) in enumerate(((own_a_ref, own_b_ref), (other_a_ref, other_b_ref))):
        scores = jnp.concatenate(
            [
                lax.dot_general(
                    q_ref[b * heads : (b + 1) * heads, :].astype(BF16),
                    (first if b < share else second)[b % share, 0],
                    LANE_CONTRACT,
                    preferred_element_type=F32,
                )
                for b in range(requests)
            ],
            axis=0,
        )
        position = (origins[block] * line + place) * span + index((flat, span), 1)
        usable = position < length_ref[...]
        scores = jnp.where(usable, scores * inv_scale, NEGATIVE)
        best = jnp.maximum(best, jnp.max(scores, axis=1, keepdims=True))
        scored.append((scores, usable, first, second))
    own_term = jnp.where(mine, jnp.exp(own_score - best), 0.0)
    norm = own_term
    weighted = own_term.astype(BF16).astype(F32) * new_value
    for scores, usable, first, second in scored:
        terms = jnp.where(usable, jnp.exp(scores - best), 0.0)
        norm = norm + jnp.sum(terms, axis=1, keepdims=True)
        weighted = weighted + jnp.concatenate(
            [
                jnp.dot(
                    terms[b * heads : (b + 1) * heads].astype(BF16),
                    (first if b < share else second)[b % share, 1],
                    preferred_element_type=F32,
                )
                for b in range(requests)
            ],
            axis=0,
        )
    o_ref[...] = weighted / jnp.where(norm > 0.0, norm, 1.0)
    blocks = []
    for i in range(heads // 2):
        first = o_ref[pl.ds(i, requests, stride=heads), :]
        second = o_ref[pl.ds(i + heads // 2, requests, stride=heads), :]
        blocks.append(jnp.where(low, first, second))
    wide = []
    for value in (best, norm):
        o_ref[...] = jnp.broadcast_to(value, (flat, LANES))
        tile = jnp.zeros((requests, LANES), F32)
        for h in range(heads):
            tile = jnp.where(lane % heads == h, o_ref[pl.ds(h, requests, stride=heads), :], tile)
        wide.append(tile)
    best_high, rest = halves(wide[0])
    best_mid, best_low = halves(rest)
    norm_high, norm_low = halves(wide[1])
    side = jnp.zeros((requests, LANES), F32)
    for k, piece in enumerate((best_high, best_mid, best_low, norm_high, norm_low)):
        side = jnp.where(lane // heads == k, piece, side)
    block = jnp.concatenate(blocks + [side], axis=0).astype(BF16)
    for peer in range(out_ref.shape[0]):
        out_ref[peer] = block


def combine_kernel(in_ref, weight_ref, out_ref):
    peers, rows, _ = in_ref.shape
    heads = SUBLANES
    half = SUBLANES
    tiles = heads // 2
    line = peers // LINES
    depth = rows - half
    flat = peers * half
    side = in_ref[:, depth:rows, :].astype(F32).reshape(flat, LANES)

    def piece(k):
        return pltpu.roll(side, LANES - heads * k, 1) if k else side

    def over_peers(reduce, value):
        return reduce(reduce(value, axis=2, keepdims=True), axis=0, keepdims=True)

    dims = (LINES // 2, 2, line, half, LANES)
    best = ((piece(0) + piece(1)) + piece(2)).reshape(dims)
    norm = (piece(3) + piece(4)).reshape(dims)
    factor = norm * jnp.exp(best - over_peers(jnp.max, best))
    factor = factor / over_peers(jnp.sum, factor)
    factor = factor.reshape(flat, LANES)
    factor = jnp.where(index((flat, LANES), 1) < heads, factor, 0.0)
    dims = (LANES, tiles * LANES)
    column = index(dims, 1)
    owner = column // LANES + tiles * (column % LANES // (LANES // 2))
    pick = (index(dims, 0) == owner).astype(F32).astype(BF16)
    high, rest = halves(factor)
    factor = jnp.dot(high.astype(BF16), pick, preferred_element_type=F32) + jnp.dot(
        rest.astype(BF16), pick, preferred_element_type=F32
    )
    weights = weight_ref[...].astype(F32)
    take = low_lanes(weights.shape[0])
    result = jnp.zeros((2 * half, LANES), F32)
    for i in range(tiles):
        averaged = [jnp.zeros((half, LANES), F32) for _ in range(2)]
        for peer in range(peers):
            parity = peer // line % 2
            averaged[parity] = averaged[parity] + in_ref[
                peer, i * half : (i + 1) * half, :
            ].astype(F32) * factor[peer * half : (peer + 1) * half, i * LANES : (i + 1) * LANES]
        first = weights[:, i // 2 * LANES : (i // 2 + 1) * LANES]
        second = weights[:, (i // 2 + 2) * LANES : (i // 2 + 3) * LANES]
        if i % 2 == 0:
            tile = jnp.where(take, first, turned(second))
        else:
            tile = jnp.where(take, turned(first), second)
        tile = jnp.concatenate([tile, tile], axis=0).astype(BF16)
        result = result + lax.dot_general(
            jnp.concatenate(averaged, axis=0).astype(BF16),
            tile,
            LANE_CONTRACT,
            preferred_element_type=F32,
        )
    outer = result[:half]
    inner = pltpu.roll(result[half:], half // 2, 0)
    upper = index((half, LANES), 0) < half // 2
    out_ref[...] = jnp.where(
        low_lanes(half), jnp.where(upper, outer, inner), jnp.where(upper, inner, outer)
    )


def unpacked(packed):
    width = LANES // 2
    return jnp.concatenate([packed[:, :width], turned(packed)[:, :width]], axis=0)


def packed_squares(packed, offset=0):
    half = packed.shape[0]
    low = low_lanes(half)
    square = packed * packed
    first = jnp.sum(jnp.where(low, square, 0.0), axis=1, keepdims=True)
    second = jnp.sum(jnp.where(low, 0.0, square), axis=1, keepdims=True)
    return to_row(first, offset) + to_row(second, offset + half)


def gate_kernel(own_ref, a_ref, b_ref, c_ref, x_ref, gain_ref, weight_ref, out_ref, one_ref):
    parts = (own_ref[...] + a_ref[...]) + (b_ref[...] + c_ref[...])
    one = (x_ref[...] + parts).astype(BF16).astype(F32)
    one_ref[...] = one
    normed = unpacked(one * gain_ref[...]).astype(BF16)
    requests = normed.shape[0]
    both = jnp.dot(normed, weight_ref[...], preferred_element_type=F32)
    width = both.shape[1] // 2
    high_part, low_part = halves(packed_squares(one))
    side = block_of([high_part, low_part]).astype(BF16)
    low = low_lanes(requests)
    for t in range(width // LANES):
        gate = both[:, t * LANES : (t + 1) * LANES]
        up = both[:, width + t * LANES : width + (t + 1) * LANES]
        out_ref[2 * t, 0:requests] = jnp.where(low, gate, turned(up)).astype(BF16)
        out_ref[2 * t + 1, 0:requests] = jnp.where(low, turned(gate), up).astype(BF16)
        out_ref[2 * t, requests : requests + SUBLANES] = side
        out_ref[2 * t + 1, requests : requests + SUBLANES] = side


def activation_kernel(in_ref, out_ref):
    total = summed(in_ref)
    requests = total.shape[0] - SUBLANES
    scale_row = norm_scale(total[requests : requests + 1] + total[requests + 1 : requests + 2])
    both = total[:requests] * to_column(scale_row, requests)
    active = both / (1.0 + jnp.exp(-both)) * turned(both)
    half = requests // 2
    packed = jnp.where(low_lanes(half), active[:half], turned(active)[half:]).astype(BF16)
    for peer in range(out_ref.shape[0]):
        out_ref[peer] = packed


def down_kernel(in_ref, weight_ref, out_ref):
    peers, half, _ = in_ref.shape
    low = low_lanes(half)
    total = jnp.zeros((2 * half, LANES), F32)
    for t in range(peers // 2):
        first = in_ref[2 * t].astype(F32)
        second = in_ref[2 * t + 1].astype(F32)
        units = jnp.concatenate(
            [jnp.where(low, first, turned(second)), jnp.where(low, turned(first), second)], axis=0
        )
        tile = weight_ref[:, t * LANES : (t + 1) * LANES]
        tile = jnp.concatenate([tile, tile], axis=0)
        total = total + lax.dot_general(
            units.astype(BF16), tile, LANE_CONTRACT, preferred_element_type=F32
        )
    out_ref[...] = jnp.where(low, total[:half], total[half:])


def next_kernel(
    guide_ref,
    own_ref,
    other_ref,
    final_ref,
    gain_ref,
    query_ref,
    pair_ref,
    out_ref,
    head_ref,
):
    guide = guide_ref[0]
    own = own_ref[...].astype(F32)
    other = other_ref[...].astype(F32)
    half = own.shape[0]
    normed = unpacked(own * gain_ref[...]).astype(BF16)
    query = jnp.dot(normed, query_ref[...], preferred_element_type=F32)
    tiles = [query[:, j * LANES : (j + 1) * LANES] for j in range(query.shape[1] // LANES)]
    tiles += pair_dots(normed, pair_ref)
    first = jnp.where(guide == 0, own, other)
    second = jnp.where(guide == 0, other, own)
    high_part, low_part = halves(packed_squares(first) + packed_squares(second, 2 * half))
    side = block_of([high_part, low_part])
    zero = jnp.zeros((half, LANES), F32)
    line = out_ref.shape[0] // LINES
    for peer in range(out_ref.shape[0]):
        j, part = divmod(peer // line // 2 * line + peer % line, 2)
        piece = tiles[j][part * half : (part + 1) * half] if j < len(tiles) else zero
        out_ref[peer] = jnp.concatenate([piece, side], axis=0).astype(BF16)
    width = LANES // 2
    both = []
    for group in (first, second):
        group = group * final_ref[...]
        both.append(jnp.where(guide == 0, group, turned(group))[:, :width])
    head_ref[...] = jnp.concatenate(both, axis=0).astype(BF16)


def windows_of(parity, starts):
    line = len(starts) // LINES
    return [start for peer, start in enumerate(starts) if peer // line % 2 == parity]


def window_rows(ref, wide_ref, rows, start, width):
    origin = start // LANES * LANES
    wide = wide_ref.shape[1]
    stop = min(origin + wide, ref.shape[1])
    value = ref[rows, origin:stop]
    if stop - origin < wide:
        wide_ref[...] = jnp.zeros(wide_ref.shape, F32)
        wide_ref[:, 0 : stop - origin] = value
        value = wide_ref[...]
    return pltpu.roll(value, (wide - start + origin) % wide, 1)[:, :width]


def share_kernel(
    spot_ref, x_ref, weight_hbm, head_ref, cond_ref, plain_ref, wide_ref, weight_ref, sems, *, starts
):
    parity = spot_ref[0]
    vocabulary = weight_ref.shape[1]
    step = vocabulary // sems.shape[0] // LANES * LANES + LANES
    cuts = [(start, min(start + step, vocabulary)) for start in range(0, vocabulary, step)]
    copies = [
        pltpu.make_async_copy(
            weight_hbm.at[:, pl.ds(start, stop - start)],
            weight_ref.at[:, pl.ds(start, stop - start)],
            sems.at[k],
        )
        for k, (start, stop) in enumerate(cuts)
    ]
    for copy in copies:
        copy.start()
    x = x_ref[...]
    for copy, (start, stop) in zip(copies, cuts):
        copy.wait()
        head_ref[:, start:stop] = jnp.dot(
            x, weight_ref[:, start:stop], preferred_element_type=F32
        )
    half = head_ref.shape[0] // 2
    width = cond_ref.shape[2]

    def write(sent):
        for slot, start in enumerate(windows_of(sent, starts)):
            for k, ref in enumerate((cond_ref, plain_ref)):
                rows = slice(k * half, (k + 1) * half)
                ref[slot] = window_rows(head_ref, wide_ref, rows, start, width).astype(BF16)

    pl.when(parity == 0)(lambda: write(1))
    pl.when(parity != 0)(lambda: write(0))


def guided_kernel(
    spot_ref, in_ref, guidance_ref, head_ref, cond_ref, plain_ref, out_ref, wide_ref, *, starts
):
    me = spot_ref[0]
    guide = spot_ref[1]
    parity = spot_ref[2]
    total = summed(in_ref)
    half = SUBLANES
    scale_row = norm_scale(total[half : half + 1] + total[half + 1 : half + 2])

    def scales(offset):
        hit = index((half, LANES), 1) == index((half, LANES), 0) + offset
        return jnp.sum(jnp.where(hit, scale_row, 0.0), axis=1, keepdims=True)

    guidance = guidance_ref[...]
    first = guidance * scales(guide * half)
    second = (1.0 - guidance) * scales(2 * half + guide * half)
    piece = (total[:half] * scales(2 * half * guide + me % 2 * half)).astype(BF16)
    width = cond_ref.shape[2]

    def write(kept):
        for slot, start in enumerate(windows_of(kept, starts)):
            cond = window_rows(head_ref, wide_ref, slice(0, half), start, width)
            plain = window_rows(head_ref, wide_ref, slice(half, 2 * half), start, width)
            cond = cond + cond_ref[slot].astype(F32)
            plain = plain + plain_ref[slot].astype(F32)
            out_ref[slot, :, 0:width] = (first * cond + second * plain).astype(BF16)
            out_ref[slot, :, width : width + LANES] = piece

    pl.when(parity == 0)(lambda: write(0))
    pl.when(parity != 0)(lambda: write(1))


def finish_kernel(in_ref, guided_ref, query_ref, pair_ref, pairs_ref):
    window = in_ref.shape[2] - LANES
    total = in_ref[0, :, 0:window].astype(F32)
    for peer in range(1, in_ref.shape[0]):
        total = total + in_ref[peer, :, 0:window].astype(F32)
    guided_ref[...] = total[:, : guided_ref.shape[1]]
    tiles = query_ref.shape[1] // LANES
    half = in_ref.shape[1]

    def tile(j):
        return jnp.concatenate(
            [in_ref[2 * j, :, window : window + LANES], in_ref[2 * j + 1, :, window : window + LANES]],
            axis=0,
        )

    for j in range(tiles):
        query_ref[:, j * LANES : (j + 1) * LANES] = tile(j)
    for which in range(2):
        pairs_ref[pl.ds(which, 2 * half, stride=2), :] = tile(tiles + which).astype(F32)
    pair_ref[...] = pairs_ref[...].astype(BF16)


def local(
    hidden,
    lengths,
    kv_cache,
    attn_gain,
    w_query,
    w_key_value,
    w_out,
    mlp_gain,
    w_gate_up,
    w_down,
    final_gain,
    w_head,
    next_gain,
    w_next_query,
    w_next_kv,
    tenant,
    guide_scale,
):
    x_rows = hidden[0]
    length = lengths[0]
    cache_block = kv_cache[0]
    requests, local_width = x_rows.shape
    half = requests // 2
    peers = lax.axis_size("row")
    me = lax.axis_index("row").astype(jnp.int32)
    guide = lax.axis_index("guide").astype(jnp.int32)

    def doubled(gain):
        gain = gain.astype(F32)
        return jnp.concatenate([gain, gain])[None, :]

    query_width = w_query.shape[1]
    line = peers // LINES
    share = requests // 4
    column = me // line
    parity = column % 2

    def quarter_of(source, which):
        return lax.dynamic_slice_in_dim(source, which * share, share, 0)

    def nearer(k):
        return k + 1 - 2 * (k % 2)

    def farther(k):
        return k - 1 + 2 * (k % 2)

    def between(block, partner):
        pairs = [(i, partner(i // line) % LINES * line + i % line) for i in range(peers)]
        return lax.ppermute(block, "row", pairs)

    sent = [quarter_of(cache_block, k) for k in (1 - parity, 2 + parity)]
    x_first, sent, cache_later = lax.optimization_barrier((x_rows, sent, cache_block))
    caches = [quarter_of(cache_later, k) for k in (parity, 3 - parity)] + [
        between(sent[0], nearer),
        between(sent[1], farther),
    ]
    depth = query_width // LANES * half
    operands = [
        pltpu.with_memory_space_constraint(operand, pltpu.HBM)
        for operand in (
            x_first,
            attn_gain[None, :],
            w_query,
            w_key_value.reshape(2 * local_width, -1),
        )
    ]
    payload = pl.pallas_call(
        start_kernel,
        out_shape=shape((peers, depth + SUBLANES, LANES), BF16),
        in_specs=[pl.BlockSpec(memory_space=pltpu.HBM)] * len(operands),
        out_specs=pl.BlockSpec(memory_space=pltpu.VMEM),
        scratch_shapes=[pltpu.VMEM(operand.shape, operand.dtype) for operand in operands]
        + [pltpu.SemaphoreType.DMA((len(operands),))],
        compiler_params=pltpu.CompilerParams(vmem_limit_bytes=8 << 20),
    )(*operands)
    arrived = exchange(payload, "row")
    my_lengths = jnp.where(
        parity == 0,
        jnp.concatenate([length[:share], length[3 * share :]]),
        length[share : 3 * share],
    )
    quarter = LANES // 4
    lane = jnp.arange(LANES)
    frequency = ROPE_BASE ** (-2.0 * (lane % quarter).astype(F32) / HD)
    angles = my_lengths.astype(F32)[:, None] * frequency[None, :]
    cosine = jnp.cos(angles)
    sine = jnp.where(lane % (2 * quarter) < quarter, -1.0, 1.0)[None, :] * jnp.sin(angles)
    flat = half * SUBLANES
    partial = call(
        attention_kernel,
        shape((peers, depth + SUBLANES, LANES), BF16),
        me[None],
        arrived,
        cosine,
        sine,
        jnp.repeat(my_lengths, SUBLANES)[:, None],
        *caches,
        scratch=[
            pltpu.VMEM((flat, LANES), F32),
            pltpu.VMEM((flat, LANES), F32),
        ],
        scalars=1,
    )
    arrived = exchange(partial, "row")
    out_part = call(combine_kernel, shape((half, LANES), F32), arrived, w_out.T)
    x_packed = jnp.concatenate([x_rows[:half], x_rows[half:]], axis=1).astype(F32)
    payload, one_packed = call(
        gate_kernel,
        (shape((peers, requests + SUBLANES, LANES), BF16), shape((half, LANES), F32)),
        out_part,
        *from_others(out_part, "col"),
        x_packed,
        doubled(mlp_gain),
        w_gate_up.reshape(local_width, -1),
    )
    arrived = exchange(payload, "row")
    active = call(activation_kernel, shape((peers, half, LANES), BF16), arrived)
    arrived = exchange(active, "row")
    down_part = call(down_kernel, shape((half, LANES), F32), arrived, w_down.T)
    a, b, c = from_others(down_part, "col")
    residual_two = (one_packed + ((down_part + a) + (b + c))).astype(BF16)
    other_two = partner_2(residual_two, "guide", 0)
    payload, head_input = call(
        next_kernel,
        (shape((peers, 2 * SUBLANES, LANES), BF16), shape((requests, local_width), BF16)),
        guide[None],
        residual_two,
        other_two,
        doubled(final_gain),
        doubled(next_gain),
        w_next_query,
        w_next_kv.reshape(2 * local_width, -1),
        scalars=1,
    )
    arrived = exchange(payload, "row")
    guidance = jnp.sum(
        jnp.where(
            tenant[:, None] == jnp.arange(TENANTS, dtype=jnp.int32)[None, :],
            guide_scale[None, :],
            0.0,
        ),
        axis=1,
    )
    my_guidance = lax.dynamic_slice_in_dim(guidance, guide * half, half, 0)[:, None]
    vocabulary = w_head.shape[1]
    part = vocabulary // peers
    width = (part + LANES - 1) // LANES * LANES
    starts = [part * k for k in range(peers)]
    wide = pltpu.VMEM((half, width + LANES), F32)
    members = peers // 2
    head_part, cond_sent, plain_sent = call(
        functools.partial(share_kernel, starts=starts),
        (
            shape((requests, vocabulary), F32),
            shape((members, half, width), BF16),
            shape((members, half, width), BF16),
        ),
        parity[None],
        head_input,
        pltpu.with_memory_space_constraint(w_head, pltpu.HBM),
        scratch=[wide, pltpu.VMEM(w_head.shape, BF16), pltpu.SemaphoreType.DMA((4,))],
        scalars=1,
        in_hbm=1,
        limit=12 << 20,
    )
    payload = call(
        functools.partial(guided_kernel, starts=starts),
        shape((members, half, width + LANES), BF16),
        jnp.stack([me, guide, parity]),
        arrived,
        my_guidance,
        head_part,
        between(cond_sent, nearer),
        between(plain_sent, farther),
        scratch=[wide],
        scalars=1,
    )
    groups = [[i for i in range(peers) if i // line % 2 == k] for k in range(2)]
    arrived = lax.all_to_all(payload, "row", 0, 0, axis_index_groups=groups, tiled=True)
    guided, next_query, next_pairs = call(
        finish_kernel,
        (
            shape((half, part), F32),
            shape((requests, query_width), BF16),
            shape((2 * requests, LANES), BF16),
        ),
        arrived,
        scratch=[pltpu.VMEM((2 * requests, LANES), F32)],
    )
    return (guided, next_query[None], next_pairs.reshape(1, requests, 2, LANES))


def solution(mesh):
    placed = (
        P("guide", None, "row"),
        P("guide", None),
        P("guide", None, None, "row", "col"),
        P("row"),
        P("row", "col"),
        P("row", None, "col"),
        P("col", "row"),
        P("row"),
        P("row", None, "col"),
        P("col", "row"),
        P("row"),
        P("row", "col"),
        P("row"),
        P("row", "col"),
        P("row", None, "col"),
        P(),
        P(),
    )
    return jax.shard_map(
        local,
        mesh=mesh,
        in_specs=placed,
        out_specs=(
            P("guide", ("col", "row")),
            P("guide", None, "col"),
            P("guide", None, None, "col"),
        ),
        check_vma=False,
    )
```

```python
import functools

import jax
import jax.numpy as jnp
from jax import lax
from jax.experimental import pallas as pl
from jax.experimental.pallas import tpu as pltpu
from jax.sharding import PartitionSpec as P

D = 2048
HEADS = 32
KVH = 8
HD = 64
TENANTS = 4
LANES = 128
SUBLANES = 8
LINES = 4

EPSILON = 1e-05
ROPE_BASE = 500000.0
NEGATIVE = -1e30

F32 = jnp.float32
BF16 = jnp.bfloat16
LANE_CONTRACT = (((1,), (1,)), ((), ()))


def exchange(x, axis):
    return lax.all_to_all(x, axis, 0, 0, tiled=True)


def partner_2(x, axis, apart):
    return lax.ppermute(x, axis, [(i, i ^ 1 << apart) for i in range(lax.axis_size(axis))])


def from_others(x, axis):
    n = lax.axis_size(axis)
    return [lax.ppermute(x, axis, [(i, (i + k) % n) for i in range(n)]) for k in range(1, n)]


def call(body, outs, *operands, scratch=(), scalars=0, in_hbm=0, limit=8 << 20):
    specs = [pl.BlockSpec(memory_space=pltpu.SMEM)] * scalars
    specs += [pl.BlockSpec(memory_space=pltpu.VMEM)] * (len(operands) - scalars - in_hbm)
    specs += [pl.BlockSpec(memory_space=pltpu.HBM)] * in_hbm
    out_specs = jax.tree.map(lambda _: pl.BlockSpec(memory_space=pltpu.VMEM), outs)
    return pl.pallas_call(
        body,
        out_shape=outs,
        in_specs=specs,
        out_specs=out_specs,
        scratch_shapes=list(scratch),
        compiler_params=pltpu.CompilerParams(vmem_limit_bytes=limit),
    )(*operands)


def shape(dims, dtype):
    return jax.ShapeDtypeStruct(dims, dtype)


def index(dims, dim):
    return lax.broadcasted_iota(jnp.int32, dims, dim)


def low_lanes(rows):
    return index((rows, LANES), 1) < LANES // 2


def turned(x):
    return pltpu.roll(x, LANES // 2, 1)


def to_row(column, offset=0):
    n = column.shape[0]
    hit = index((n, LANES), 1) == index((n, LANES), 0) + offset
    return jnp.sum(jnp.where(hit, column, 0.0), axis=0, keepdims=True)


def to_column(row, n, offset=0):
    hit = index((n, LANES), 1) == index((n, LANES), 0) + offset
    return jnp.sum(jnp.where(hit, row, 0.0), axis=1, keepdims=True)


def halves(value):
    high = value.astype(BF16).astype(F32)
    return high, value - high


def block_of(rows):
    at = index((SUBLANES, LANES), 0)
    block = jnp.zeros((SUBLANES, LANES), F32)
    for k, row in enumerate(rows):
        block = jnp.where(at == k, row, block)
    return block


def summed(ref):
    total = ref[0].astype(F32)
    for k in range(1, ref.shape[0]):
        total = total + ref[k].astype(F32)
    return total


def norm_scale(total):
    return lax.rsqrt(total / D + EPSILON)


def spread(normed, which):
    width = normed.shape[1]
    dims = (width, 2 * width)
    pick = (index(dims, 1) == 2 * index(dims, 0) + which).astype(F32).astype(BF16)
    return jnp.dot(normed, pick, preferred_element_type=F32).astype(BF16)


def pair_dots(normed, pair_ref):
    weights = pair_ref[...]
    return [jnp.dot(spread(normed, w), weights, preferred_element_type=F32) for w in range(2)]


def start_kernel(
    x_hbm, gain_hbm, query_hbm, pair_hbm, out_ref, x_ref, gain_ref, query_ref, pair_ref, sems
):
    sources = (x_hbm, gain_hbm, query_hbm, pair_hbm)
    targets = (x_ref, gain_ref, query_ref, pair_ref)
    copies = [
        pltpu.make_async_copy(source, target, sems.at[k])
        for k, (source, target) in enumerate(zip(sources, targets))
    ]
    for copy in copies:
        copy.start()
    for copy in copies:
        copy.wait()
    x = x_ref[...].astype(F32)
    requests = x.shape[0]
    normed = (x * gain_ref[...].astype(F32)).astype(BF16)
    query = jnp.dot(normed, query_ref[...], preferred_element_type=F32)
    keys, values = pair_dots(normed, pair_ref)
    low = low_lanes(requests)
    own = (jnp.where(low, keys, turned(values)), jnp.where(low, turned(keys), values))
    high_part, low_part = halves(to_row(jnp.sum(x * x, axis=1, keepdims=True)))
    half = requests // 2
    upper = index((half, LANES), 0) < half // 2
    variants = []
    for parity in range(2):
        pieces = []
        for tile in range(query.shape[1] // LANES):
            first = query[:half, tile * LANES : (tile + 1) * LANES]
            second = query[half:, tile * LANES : (tile + 1) * LANES]
            if parity:
                first = pltpu.roll(first, half // 2, 0)
                second = pltpu.roll(second, half // 2, 0)
            pieces.append(jnp.where(upper, first, second))
        variants.append(jnp.concatenate(pieces, axis=0).astype(BF16))
    depth = variants[0].shape[0]
    line = out_ref.shape[0] // LINES
    for peer in range(out_ref.shape[0]):
        column, place = divmod(peer, line)
        quarter = column % 2 if column < 2 else 3 - column % 2
        request = quarter * (requests // 4) + place // 2
        side = block_of([own[place % 2][request : request + 1], high_part, low_part])
        out_ref[peer, 0:depth] = variants[column % 2]
        out_ref[peer, depth : depth + SUBLANES] = side.astype(BF16)


def turn_pairs(x, cosine, sine):
    quarter = LANES // 4
    first = index(x.shape, 1) % (2 * quarter) < quarter
    other = jnp.where(first, pltpu.roll(x, 3 * quarter, 1), pltpu.roll(x, quarter, 1))
    return x * cosine + other * sine


def attention_kernel(
    me_ref,
    in_ref,
    cos_ref,
    sin_ref,
    length_ref,
    own_a_ref,
    own_b_ref,
    other_a_ref,
    other_b_ref,
    out_ref,
    q_ref,
    o_ref,
):
    share, _, span, _ = own_a_ref.shape
    heads = SUBLANES
    requests = 2 * share
    line = in_ref.shape[0] // LINES
    column = me_ref[0] // line
    place = me_ref[0] % line
    parity = column % 2
    total = summed(in_ref)
    depth = total.shape[0] - SUBLANES
    scale_row = norm_scale(total[depth + 1 : depth + 2] + total[depth + 2 : depth + 3])
    lane = index((requests, LANES), 1)
    row = index((requests, LANES), 0)
    wanted = jnp.where(row < share, parity * share + row, (2 - parity) * share + row)
    scale = jnp.sum(jnp.where(lane == wanted, scale_row, 0.0), axis=1, keepdims=True)
    cosine = cos_ref[...]
    sine = sin_ref[...]
    low = low_lanes(requests)
    tiles = depth // requests
    for j in range(tiles):
        tile = total[j * requests : (j + 1) * requests] * scale
        tile = turn_pairs(tile, cosine, sine).astype(BF16).astype(F32)
        other = turned(tile)
        if j < tiles // 2:
            even, odd = jnp.where(low, tile, 0.0), jnp.where(low, other, 0.0)
        else:
            even, odd = jnp.where(low, 0.0, other), jnp.where(low, 0.0, tile)
        q_ref[pl.ds(2 * j, requests, stride=heads), :] = even
        q_ref[pl.ds(2 * j + 1, requests, stride=heads), :] = odd
    own_request = column // 2 * share + place // 2
    own_head = place % 2
    one_low = low_lanes(1)
    pick = row == own_request
    own_scale = jnp.sum(jnp.where(pick[:, :1], scale, 0.0), axis=0, keepdims=True)
    own_pair = total[depth : depth + 1] * own_scale
    own_cos = jnp.sum(jnp.where(pick, cosine, 0.0), axis=0, keepdims=True)
    own_sin = jnp.sum(jnp.where(pick, sine, 0.0), axis=0, keepdims=True)
    new_key = jnp.where(one_low, turn_pairs(own_pair, own_cos, own_sin), 0.0)
    new_value = jnp.where(one_low, 0.0, own_pair)
    new_key = jnp.where(own_head == 0, new_key, turned(new_key)).astype(BF16).astype(F32)
    new_value = jnp.where(own_head == 0, turned(new_value), new_value).astype(BF16).astype(F32)
    inv_scale = HD ** (-0.5)
    flat = requests * heads
    flat_row = index((flat, 1), 0)
    mine = (flat_row // heads == own_request) & (flat_row % heads // (heads // 2) == own_head)
    own_score = jnp.sum(q_ref[...] * new_key, axis=1, keepdims=True) * inv_scale
    own_score = jnp.where(mine, own_score, NEGATIVE)
    near = column + 1 - 2 * parity
    far = lax.rem(column + LINES - 1 + 2 * parity, LINES)
    origins = (
        jnp.broadcast_to(column, (flat, 1)),
        jnp.where(flat_row < flat // 2, near, far),
    )
    best = own_score
    scored = []
    for block, (first, second) in enumerate(((own_a_ref, own_b_ref), (other_a_ref, other_b_ref))):
        scores = jnp.concatenate(
            [
                lax.dot_general(
                    q_ref[b * heads : (b + 1) * heads, :].astype(BF16),
                    (first if b < share else second)[b % share, 0],
                    LANE_CONTRACT,
                    preferred_element_type=F32,
                )
                for b in range(requests)
            ],
            axis=0,
        )
        position = (origins[block] * line + place) * span + index((flat, span), 1)
        usable = position < length_ref[...]
        scores = jnp.where(usable, scores * inv_scale, NEGATIVE)
        best = jnp.maximum(best, jnp.max(scores, axis=1, keepdims=True))
        scored.append((scores, usable, first, second))
    own_term = jnp.where(mine, jnp.exp(own_score - best), 0.0)
    norm = own_term
    weighted = own_term.astype(BF16).astype(F32) * new_value
    for scores, usable, first, second in scored:
        terms = jnp.where(usable, jnp.exp(scores - best), 0.0)
        norm = norm + jnp.sum(terms, axis=1, keepdims=True)
        weighted = weighted + jnp.concatenate(
            [
                jnp.dot(
                    terms[b * heads : (b + 1) * heads].astype(BF16),
                    (first if b < share else second)[b % share, 1],
                    preferred_element_type=F32,
                )
                for b in range(requests)
            ],
            axis=0,
        )
    o_ref[...] = weighted / jnp.where(norm > 0.0, norm, 1.0)
    blocks = []
    for i in range(heads // 2):
        first = o_ref[pl.ds(i, requests, stride=heads), :]
        second = o_ref[pl.ds(i + heads // 2, requests, stride=heads), :]
        blocks.append(jnp.where(low, first, second))
    wide = []
    for value in (best, norm):
        o_ref[...] = jnp.broadcast_to(value, (flat, LANES))
        tile = jnp.zeros((requests, LANES), F32)
        for h in range(heads):
            tile = jnp.where(lane % heads == h, o_ref[pl.ds(h, requests, stride=heads), :], tile)
        wide.append(tile)
    best_high, rest = halves(wide[0])
    best_mid, best_low = halves(rest)
    norm_high, norm_low = halves(wide[1])
    side = jnp.zeros((requests, LANES), F32)
    for k, piece in enumerate((best_high, best_mid, best_low, norm_high, norm_low)):
        side = jnp.where(lane // heads == k, piece, side)
    block = jnp.concatenate(blocks + [side], axis=0).astype(BF16)
    for peer in range(out_ref.shape[0]):
        out_ref[peer] = block


def combine_kernel(in_ref, weight_ref, out_ref):
    peers, rows, _ = in_ref.shape
    heads = SUBLANES
    half = SUBLANES
    tiles = heads // 2
    line = peers // LINES
    depth = rows - half
    flat = peers * half
    side = in_ref[:, depth:rows, :].astype(F32).reshape(flat, LANES)

    def piece(k):
        return pltpu.roll(side, LANES - heads * k, 1) if k else side

    def over_peers(reduce, value):
        return reduce(reduce(value, axis=2, keepdims=True), axis=0, keepdims=True)

    dims = (LINES // 2, 2, line, half, LANES)
    best = ((piece(0) + piece(1)) + piece(2)).reshape(dims)
    norm = (piece(3) + piece(4)).reshape(dims)
    factor = norm * jnp.exp(best - over_peers(jnp.max, best))
    factor = factor / over_peers(jnp.sum, factor)
    factor = factor.reshape(flat, LANES)
    factor = jnp.where(index((flat, LANES), 1) < heads, factor, 0.0)
    dims = (LANES, tiles * LANES)
    column = index(dims, 1)
    owner = column // LANES + tiles * (column % LANES // (LANES // 2))
    pick = (index(dims, 0) == owner).astype(F32).astype(BF16)
    high, rest = halves(factor)
    factor = jnp.dot(high.astype(BF16), pick, preferred_element_type=F32) + jnp.dot(
        rest.astype(BF16), pick, preferred_element_type=F32
    )
    weights = weight_ref[...].astype(F32)
    take = low_lanes(weights.shape[0])
    result = jnp.zeros((2 * half, LANES), F32)
    for i in range(tiles):
        averaged = [jnp.zeros((half, LANES), F32) for _ in range(2)]
        for peer in range(peers):
            parity = peer // line % 2
            averaged[parity] = averaged[parity] + in_ref[
                peer, i * half : (i + 1) * half, :
            ].astype(F32) * factor[peer * half : (peer + 1) * half, i * LANES : (i + 1) * LANES]
        first = weights[:, i // 2 * LANES : (i // 2 + 1) * LANES]
        second = weights[:, (i // 2 + 2) * LANES : (i // 2 + 3) * LANES]
        if i % 2 == 0:
            tile = jnp.where(take, first, turned(second))
        else:
            tile = jnp.where(take, turned(first), second)
        tile = jnp.concatenate([tile, tile], axis=0).astype(BF16)
        result = result + lax.dot_general(
            jnp.concatenate(averaged, axis=0).astype(BF16),
            tile,
            LANE_CONTRACT,
            preferred_element_type=F32,
        )
    outer = result[:half]
    inner = pltpu.roll(result[half:], half // 2, 0)
    upper = index((half, LANES), 0) < half // 2
    out_ref[...] = jnp.where(
        low_lanes(half), jnp.where(upper, outer, inner), jnp.where(upper, inner, outer)
    )


def unpacked(packed):
    width = LANES // 2
    return jnp.concatenate([packed[:, :width], turned(packed)[:, :width]], axis=0)


def packed_squares(packed, offset=0):
    half = packed.shape[0]
    low = low_lanes(half)
    square = packed * packed
    first = jnp.sum(jnp.where(low, square, 0.0), axis=1, keepdims=True)
    second = jnp.sum(jnp.where(low, 0.0, square), axis=1, keepdims=True)
    return to_row(first, offset) + to_row(second, offset + half)


def gate_kernel(own_ref, a_ref, b_ref, c_ref, x_ref, gain_ref, weight_ref, out_ref, one_ref):
    parts = (own_ref[...] + a_ref[...]) + (b_ref[...] + c_ref[...])
    one = (x_ref[...] + parts).astype(BF16).astype(F32)
    one_ref[...] = one
    normed = unpacked(one * gain_ref[...]).astype(BF16)
    requests = normed.shape[0]
    both = jnp.dot(normed, weight_ref[...], preferred_element_type=F32)
    width = both.shape[1] // 2
    high_part, low_part = halves(packed_squares(one))
    side = block_of([high_part, low_part]).astype(BF16)
    low = low_lanes(requests)
    for t in range(width // LANES):
        gate = both[:, t * LANES : (t + 1) * LANES]
        up = both[:, width + t * LANES : width + (t + 1) * LANES]
        out_ref[2 * t, 0:requests] = jnp.where(low, gate, turned(up)).astype(BF16)
        out_ref[2 * t + 1, 0:requests] = jnp.where(low, turned(gate), up).astype(BF16)
        out_ref[2 * t, requests : requests + SUBLANES] = side
        out_ref[2 * t + 1, requests : requests + SUBLANES] = side


def activation_kernel(in_ref, out_ref):
    total = summed(in_ref)
    requests = total.shape[0] - SUBLANES
    scale_row = norm_scale(total[requests : requests + 1] + total[requests + 1 : requests + 2])
    both = total[:requests] * to_column(scale_row, requests)
    active = both / (1.0 + jnp.exp(-both)) * turned(both)
    half = requests // 2
    packed = jnp.where(low_lanes(half), active[:half], turned(active)[half:]).astype(BF16)
    for peer in range(out_ref.shape[0]):
        out_ref[peer] = packed


def down_kernel(in_ref, weight_ref, out_ref):
    peers, half, _ = in_ref.shape
    low = low_lanes(half)
    total = jnp.zeros((2 * half, LANES), F32)
    for t in range(peers // 2):
        first = in_ref[2 * t].astype(F32)
        second = in_ref[2 * t + 1].astype(F32)
        units = jnp.concatenate(
            [jnp.where(low, first, turned(second)), jnp.where(low, turned(first), second)], axis=0
        )
        tile = weight_ref[:, t * LANES : (t + 1) * LANES]
        tile = jnp.concatenate([tile, tile], axis=0)
        total = total + lax.dot_general(
            units.astype(BF16), tile, LANE_CONTRACT, preferred_element_type=F32
        )
    out_ref[...] = jnp.where(low, total[:half], total[half:])


def next_kernel(
    guide_ref,
    own_ref,
    other_ref,
    final_ref,
    gain_ref,
    query_ref,
    pair_ref,
    out_ref,
    head_ref,
):
    guide = guide_ref[0]
    own = own_ref[...].astype(F32)
    other = other_ref[...].astype(F32)
    half = own.shape[0]
    normed = unpacked(own * gain_ref[...]).astype(BF16)
    query = jnp.dot(normed, query_ref[...], preferred_element_type=F32)
    tiles = [query[:, j * LANES : (j + 1) * LANES] for j in range(query.shape[1] // LANES)]
    tiles += pair_dots(normed, pair_ref)
    first = jnp.where(guide == 0, own, other)
    second = jnp.where(guide == 0, other, own)
    high_part, low_part = halves(packed_squares(first) + packed_squares(second, 2 * half))
    side = block_of([high_part, low_part])
    zero = jnp.zeros((half, LANES), F32)
    line = out_ref.shape[0] // LINES
    for peer in range(out_ref.shape[0]):
        j, part = divmod(peer // line // 2 * line + peer % line, 2)
        piece = tiles[j][part * half : (part + 1) * half] if j < len(tiles) else zero
        out_ref[peer] = jnp.concatenate([piece, side], axis=0).astype(BF16)
    width = LANES // 2
    both = []
    for group in (first, second):
        group = group * final_ref[...]
        both.append(jnp.where(guide == 0, group, turned(group))[:, :width])
    head_ref[...] = jnp.concatenate(both, axis=0).astype(BF16)


def windows_of(parity, starts):
    line = len(starts) // LINES
    return [start for peer, start in enumerate(starts) if peer // line % 2 == parity]


def window_rows(ref, wide_ref, rows, start, width):
    origin = start // LANES * LANES
    wide = wide_ref.shape[1]
    stop = min(origin + wide, ref.shape[1])
    value = ref[rows, origin:stop]
    if stop - origin < wide:
        wide_ref[...] = jnp.zeros(wide_ref.shape, F32)
        wide_ref[:, 0 : stop - origin] = value
        value = wide_ref[...]
    return pltpu.roll(value, (wide - start + origin) % wide, 1)[:, :width]


def share_kernel(
    spot_ref, x_ref, weight_hbm, head_ref, cond_ref, plain_ref, wide_ref, weight_ref, sems, *, starts
):
    parity = spot_ref[0]
    vocabulary = weight_ref.shape[1]
    step = vocabulary // sems.shape[0] // LANES * LANES + LANES
    cuts = [(start, min(start + step, vocabulary)) for start in range(0, vocabulary, step)]
    copies = [
        pltpu.make_async_copy(
            weight_hbm.at[:, pl.ds(start, stop - start)],
            weight_ref.at[:, pl.ds(start, stop - start)],
            sems.at[k],
        )
        for k, (start, stop) in enumerate(cuts)
    ]
    for copy in copies:
        copy.start()
    x = x_ref[...]
    for copy, (start, stop) in zip(copies, cuts):
        copy.wait()
        head_ref[:, start:stop] = jnp.dot(
            x, weight_ref[:, start:stop], preferred_element_type=F32
        )
    half = head_ref.shape[0] // 2
    width = cond_ref.shape[2]

    def write(sent):
        for slot, start in enumerate(windows_of(sent, starts)):
            for k, ref in enumerate((cond_ref, plain_ref)):
                rows = slice(k * half, (k + 1) * half)
                ref[slot] = window_rows(head_ref, wide_ref, rows, start, width).astype(BF16)

    pl.when(parity == 0)(lambda: write(1))
    pl.when(parity != 0)(lambda: write(0))


def guided_kernel(
    spot_ref, in_ref, guidance_ref, head_ref, cond_ref, plain_ref, out_ref, wide_ref, *, starts
):
    me = spot_ref[0]
    guide = spot_ref[1]
    parity = spot_ref[2]
    total = summed(in_ref)
    half = SUBLANES
    scale_row = norm_scale(total[half : half + 1] + total[half + 1 : half + 2])

    def scales(offset):
        hit = index((half, LANES), 1) == index((half, LANES), 0) + offset
        return jnp.sum(jnp.where(hit, scale_row, 0.0), axis=1, keepdims=True)

    guidance = guidance_ref[...]
    first = guidance * scales(guide * half)
    second = (1.0 - guidance) * scales(2 * half + guide * half)
    piece = (total[:half] * scales(2 * half * guide + me % 2 * half)).astype(BF16)
    width = cond_ref.shape[2]

    def write(kept):
        for slot, start in enumerate(windows_of(kept, starts)):
            cond = window_rows(head_ref, wide_ref, slice(0, half), start, width)
            plain = window_rows(head_ref, wide_ref, slice(half, 2 * half), start, width)
            cond = cond + cond_ref[slot].astype(F32)
            plain = plain + plain_ref[slot].astype(F32)
            out_ref[slot, :, 0:width] = (first * cond + second * plain).astype(BF16)
            out_ref[slot, :, width : width + LANES] = piece

    pl.when(parity == 0)(lambda: write(0))
    pl.when(parity != 0)(lambda: write(1))


def finish_kernel(in_ref, guided_ref, query_ref, pair_ref, pairs_ref):
    window = in_ref.shape[2] - LANES
    total = in_ref[0, :, 0:window].astype(F32)
    for peer in range(1, in_ref.shape[0]):
        total = total + in_ref[peer, :, 0:window].astype(F32)
    guided_ref[...] = total[:, : guided_ref.shape[1]]
    tiles = query_ref.shape[1] // LANES
    half = in_ref.shape[1]

    def tile(j):
        return jnp.concatenate(
            [in_ref[2 * j, :, window : window + LANES], in_ref[2 * j + 1, :, window : window + LANES]],
            axis=0,
        )

    for j in range(tiles):
        query_ref[:, j * LANES : (j + 1) * LANES] = tile(j)
    for which in range(2):
        pairs_ref[pl.ds(which, 2 * half, stride=2), :] = tile(tiles + which).astype(F32)
    pair_ref[...] = pairs_ref[...].astype(BF16)


def local(
    hidden,
    lengths,
    kv_cache,
    attn_gain,
    w_query,
    w_key_value,
    w_out,
    mlp_gain,
    w_gate_up,
    w_down,
    final_gain,
    w_head,
    next_gain,
    w_next_query,
    w_next_kv,
    tenant,
    guide_scale,
):
    x_rows = hidden[0]
    length = lengths[0]
    cache_block = kv_cache[0]
    requests, local_width = x_rows.shape
    half = requests // 2
    peers = lax.axis_size("row")
    me = lax.axis_index("row").astype(jnp.int32)
    guide = lax.axis_index("guide").astype(jnp.int32)

    def doubled(gain):
        gain = gain.astype(F32)
        return jnp.concatenate([gain, gain])[None, :]

    query_width = w_query.shape[1]
    line = peers // LINES
    share = requests // 4
    column = me // line
    parity = column % 2

    def quarter_of(source, which):
        return lax.dynamic_slice_in_dim(source, which * share, share, 0)

    def nearer(k):
        return k + 1 - 2 * (k % 2)

    def farther(k):
        return k - 1 + 2 * (k % 2)

    def between(block, partner):
        pairs = [(i, partner(i // line) % LINES * line + i % line) for i in range(peers)]
        return lax.ppermute(block, "row", pairs)

    sent = [quarter_of(cache_block, k) for k in (1 - parity, 2 + parity)]
    x_first, sent, cache_later = lax.optimization_barrier((x_rows, sent, cache_block))
    caches = [quarter_of(cache_later, k) for k in (parity, 3 - parity)] + [
        between(sent[0], nearer),
        between(sent[1], farther),
    ]
    depth = query_width // LANES * half
    operands = [
        pltpu.with_memory_space_constraint(operand, pltpu.HBM)
        for operand in (
            x_first,
            attn_gain[None, :],
            w_query,
            w_key_value.reshape(2 * local_width, -1),
        )
    ]
    payload = pl.pallas_call(
        start_kernel,
        out_shape=shape((peers, depth + SUBLANES, LANES), BF16),
        in_specs=[pl.BlockSpec(memory_space=pltpu.HBM)] * len(operands),
        out_specs=pl.BlockSpec(memory_space=pltpu.VMEM),
        scratch_shapes=[pltpu.VMEM(operand.shape, operand.dtype) for operand in operands]
        + [pltpu.SemaphoreType.DMA((len(operands),))],
        compiler_params=pltpu.CompilerParams(vmem_limit_bytes=8 << 20),
    )(*operands)
    arrived = exchange(payload, "row")
    my_lengths = jnp.where(
        parity == 0,
        jnp.concatenate([length[:share], length[3 * share :]]),
        length[share : 3 * share],
    )
    quarter = LANES // 4
    lane = jnp.arange(LANES)
    frequency = ROPE_BASE ** (-2.0 * (lane % quarter).astype(F32) / HD)
    angles = my_lengths.astype(F32)[:, None] * frequency[None, :]
    cosine = jnp.cos(angles)
    sine = jnp.where(lane % (2 * quarter) < quarter, -1.0, 1.0)[None, :] * jnp.sin(angles)
    flat = half * SUBLANES
    partial = call(
        attention_kernel,
        shape((peers, depth + SUBLANES, LANES), BF16),
        me[None],
        arrived,
        cosine,
        sine,
        jnp.repeat(my_lengths, SUBLANES)[:, None],
        *caches,
        scratch=[
            pltpu.VMEM((flat, LANES), F32),
            pltpu.VMEM((flat, LANES), F32),
        ],
        scalars=1,
    )
    arrived = exchange(partial, "row")
    out_part = call(combine_kernel, shape((half, LANES), F32), arrived, w_out.T)
    x_packed = jnp.concatenate([x_rows[:half], x_rows[half:]], axis=1).astype(F32)
    payload, one_packed = call(
        gate_kernel,
        (shape((peers, requests + SUBLANES, LANES), BF16), shape((half, LANES), F32)),
        out_part,
        *from_others(out_part, "col"),
        x_packed,
        doubled(mlp_gain),
        w_gate_up.reshape(local_width, -1),
    )
    arrived = exchange(payload, "row")
    active = call(activation_kernel, shape((peers, half, LANES), BF16), arrived)
    arrived = exchange(active, "row")
    down_part = call(down_kernel, shape((half, LANES), F32), arrived, w_down.T)
    a, b, c = from_others(down_part, "col")
    residual_two = (one_packed + ((down_part + a) + (b + c))).astype(BF16)
    other_two = partner_2(residual_two, "guide", 0)
    payload, head_input = call(
        next_kernel,
        (shape((peers, 2 * SUBLANES, LANES), BF16), shape((requests, local_width), BF16)),
        guide[None],
        residual_two,
        other_two,
        doubled(final_gain),
        doubled(next_gain),
        w_next_query,
        w_next_kv.reshape(2 * local_width, -1),
        scalars=1,
    )
    arrived = exchange(payload, "row")
    guidance = jnp.sum(
        jnp.where(
            tenant[:, None] == jnp.arange(TENANTS, dtype=jnp.int32)[None, :],
            guide_scale[None, :],
            0.0,
        ),
        axis=1,
    )
    my_guidance = lax.dynamic_slice_in_dim(guidance, guide * half, half, 0)[:, None]
    vocabulary = w_head.shape[1]
    part = vocabulary // peers
    width = (part + LANES - 1) // LANES * LANES
    starts = [part * k for k in range(peers)]
    wide = pltpu.VMEM((half, width + LANES), F32)
    members = peers // 2
    head_part, cond_sent, plain_sent = call(
        functools.partial(share_kernel, starts=starts),
        (
            shape((requests, vocabulary), F32),
            shape((members, half, width), BF16),
            shape((members, half, width), BF16),
        ),
        parity[None],
        head_input,
        pltpu.with_memory_space_constraint(w_head, pltpu.HBM),
        scratch=[wide, pltpu.VMEM(w_head.shape, BF16), pltpu.SemaphoreType.DMA((8,))],
        scalars=1,
        in_hbm=1,
        limit=12 << 20,
    )
    payload = call(
        functools.partial(guided_kernel, starts=starts),
        shape((members, half, width + LANES), BF16),
        jnp.stack([me, guide, parity]),
        arrived,
        my_guidance,
        head_part,
        between(cond_sent, nearer),
        between(plain_sent, farther),
        scratch=[wide],
        scalars=1,
    )
    groups = [[i for i in range(peers) if i // line % 2 == k] for k in range(2)]
    arrived = lax.all_to_all(payload, "row", 0, 0, axis_index_groups=groups, tiled=True)
    guided, next_query, next_pairs = call(
        finish_kernel,
        (
            shape((half, part), F32),
            shape((requests, query_width), BF16),
            shape((2 * requests, LANES), BF16),
        ),
        arrived,
        scratch=[pltpu.VMEM((2 * requests, LANES), F32)],
    )
    return (guided, next_query[None], next_pairs.reshape(1, requests, 2, LANES))


def solution(mesh):
    placed = (
        P("guide", None, "row"),
        P("guide", None),
        P("guide", None, None, "row", "col"),
        P("row"),
        P("row", "col"),
        P("row", None, "col"),
        P("col", "row"),
        P("row"),
        P("row", None, "col"),
        P("col", "row"),
        P("row"),
        P("row", "col"),
        P("row"),
        P("row", "col"),
        P("row", None, "col"),
        P(),
        P(),
    )
    return jax.shard_map(
        local,
        mesh=mesh,
        in_specs=placed,
        out_specs=(
            P("guide", ("col", "row")),
            P("guide", None, "col"),
            P("guide", None, None, "col"),
        ),
        check_vma=False,
    )
```
